32 devices in a mesh: groups: 2 (over y), tiles: 4 (over z), rows: 2 (over x), chan: 2 (over core).
Axes of the slice: x: 2, y: 2, z: 4, core: 2. Of those that a mesh axis runs over, the one named last changes fastest.
Arguments:
- acts: bfloat16 [96, 24576], P(('groups', 'rows'), 'tiles'), parts along dimension 0, may hold values from -6 to 6
- shift: float32 [128], replicated, may hold values from -3 to 3
- weight_one: bfloat16 [3, 3, 64, 128], replicated, may hold values from -0.25 to 0.25
- weight_two: bfloat16 [3, 3, 128, 128], P(None, None, None, 'chan'), may hold values from -0.1875 to 0.1875
- cotangent: bfloat16 [48, 192, 128], P(('groups', 'rows'), 'tiles', 'chan'), parts along dimension 0, may hold values from -6 to 6
- tissue_count: int32 [4, 4], P(('groups', 'rows'), 'tiles'), parts along dimension 0, may hold values from 1 to 16, 32 in all within a row
- tile_order: int32 [4, 4, 16], P(('groups', 'rows'), 'tiles'), parts along dimension 0, may hold values from 0 to 15, each once within a row
Outputs:
- input_grad: bfloat16 [96, 24576], P(('groups', 'rows'), 'tiles'), parts along dimension 0
- first_grad: float32 [6, 3, 64, 128], P('groups', None, None, 'chan'), parts along dimension 0
- second_grad: float32 [6, 3, 128, 128], P('groups', None, None, 'chan'), parts along dimension 0
The draws below stay inside these ranges and needn't reach their ends.
There are 2 independent parts, one for each index of `groups`. The reference program is written for one: setup_inputs(seed, part) draws one part's arguments, and reference() takes and returns one part's arrays. A program takes and returns all parts, laid end to end along the dimension named above; an argument that names none is the same for every part. Nothing has to cross between parts.
Inputs may be any that keep to these rules, and one draw needn't show every extreme that they name: `tissue_count`: in each block of tile rows the counts add up to exactly 32, and some device there holds 16 tissue tiles. `tile_order`: each device's list names each of its 16 tiles once.
All inputs are finite; a program needn't handle non-finite values.
Results may differ from the reference program's by a relative error of at most 0.015.
Values may be sent and summed in bfloat16 or wider, within the bound.
No kernel may reach another device: no remote copies, remote signals or barrier semaphores. Data moves between devices by JAX's collectives and lax.ppermute only.
A program may use at most 64 MiB of HBM per device.

```python
import math
import jax
import jax.numpy as jnp
import numpy as np
from jax import lax

CIN = 64
CMID = 128
COUT = 128
TP = 12
BR = 2
BC = 8
OWN = 16
TISSUE = 32
SH = 48
SW = 384
PIXELS = 2304
N_TILES = 4
N_ROWS = 2


def block_levels(own_key, shape, shards, low, high):
    level, own = 1.0, jax.random.fold_in(own_key, 6)
    for position, blocks in shards:
        heights = jnp.exp(jax.random.uniform(jax.random.fold_in(own, position), (blocks,), jnp.float32, low / len(shards), high / len(shards)))
        level = level * jnp.repeat(heights, shape[position] // blocks).reshape([-1 if axis == position else 1 for axis in range(len(shape))])
    return level


def profile(count, total, bound, lean):
    weights = [(1 << 20) // math.isqrt(standing ** lean) + 1 for standing in range(2, count + 1)]
    rest, given = total - bound - (count - 1), [1] * (count - 1)
    while rest > 0:
        free = [i for i in range(count - 1) if given[i] < bound]
        whole, remaining = sum([weights[i] for i in free]), rest
        for i in free:
            addition = min(bound - given[i], max(1, remaining * weights[i] // whole), rest)
            given[i] = given[i] + addition
            rest = rest - addition
    return np.array([bound] + given)


def ragged_sizes(own_key, count, total, limit, skew):
    if count == 2:
        one = jax.random.randint(own_key, (), max(1, total - limit), min(limit, total - 1) + 1)
        return jnp.stack([one, total - one])
    sizes = jnp.asarray(profile(count, total, limit, skew), jnp.int32)
    twos = (count - 1) // 2
    donor, taker = sizes[1:1 + 2 * twos:2], sizes[2:2 + 2 * twos:2]
    margin = jnp.minimum(donor - 1, limit - taker)
    passed = jax.random.randint(jax.random.fold_in(own_key, 1), (twos,), 0, 1 << 20) % (margin + 1)
    sizes = sizes.at[1:1 + 2 * twos:2].set(donor - passed).at[2:2 + 2 * twos:2].set(taker + passed)
    return sizes[jax.random.permutation(jax.random.fold_in(own_key, 2), count)]


def bell_draw(key, dims, deviation, bound, split=(), held_as=jnp.bfloat16):
    loudness = block_levels(key, dims, split, -0.22, 0.18) if split else 1.0
    entries = jax.random.normal(key, dims, jnp.float32) * deviation * loudness
    return jnp.minimum(jnp.maximum(entries, -bound), bound).astype(held_as)


def setup_inputs(seed: int = 0, part: int = 0) -> dict:
    key_of = jax.random.split(jax.random.key(seed), 8)
    own_keys = jax.random.split(jax.random.fold_in(key_of[7], part), 8)
    acts = bell_draw(own_keys[0], (SH, SW * CIN), 1.0, 6.0, ((0, 2), (1, 4)))
    shift = bell_draw(key_of[1], (CMID,), 0.5, 3.0, (), jnp.float32)
    weight_one = bell_draw(key_of[2], (3, 3, CIN, CMID), (9 * CIN) ** -0.5, 0.25)
    weight_two = bell_draw(key_of[3], (3, 3, CMID, COUT), (9 * CMID) ** -0.5, 0.1875, ((3, 2),))
    cotangent = bell_draw(own_keys[4], (SH // 2, SW // 2, COUT), 1.0, 6.0, ((0, 2), (1, 4), (2, 2)))
    tissue_count = jax.vmap(lambda own: ragged_sizes(own, N_TILES, TISSUE, OWN, 2))(jax.random.split(own_keys[5], N_ROWS)).reshape((N_ROWS, N_TILES)).astype(jnp.int32)
    tile_order = jax.vmap(lambda own: jax.random.permutation(own, OWN))(jax.random.split(own_keys[6], N_ROWS * N_TILES)).reshape((N_ROWS, N_TILES, OWN)).astype(jnp.int32)
    return {"acts": acts, "shift": shift, "weight_one": weight_one, "weight_two": weight_two, "cotangent": cotangent, "tissue_count": tissue_count, "tile_order": tile_order}


def stride_conv(source, kernel):
    return lax.conv_general_dilated(source, kernel, (2, 2), ((1, 1), (1, 1)), dimension_numbers=('NHWC', 'HWIO', 'NHWC'), precision=lax.Precision.HIGHEST)

def spread_conv(source, kernel):
    return lax.conv_general_dilated(source, kernel, (1, 1), ((2, 2), (2, 2)), rhs_dilation=(2, 2), dimension_numbers=('NHWC', 'HWIO', 'NHWC'), precision=lax.Precision.HIGHEST)

def reference(acts, shift, weight_one, weight_two, cotangent, tissue_count, tile_order):
    picture = acts.reshape(1, SH, SW, CIN).astype(jnp.float32)
    first = weight_one.astype(jnp.float32)
    second = weight_two.astype(jnp.float32)
    pre = stride_conv(picture, first) + shift
    middle = jnp.maximum(pre, 0.0).astype(jnp.bfloat16)
    ranks = jnp.arange(OWN, dtype=jnp.int32)
    hits = (tile_order[:, :, :, None] == ranks) & (ranks[:, None] < tissue_count[:, :, None, None])
    tissue = lax.optimization_barrier(jnp.sum(hits.astype(jnp.int32), axis=2))
    grid = tissue.reshape(N_ROWS, N_TILES, BR, BC).transpose(0, 2, 1, 3).reshape(N_ROWS * BR, N_TILES * BC)
    pixel_mask = jnp.repeat(jnp.repeat(grid, TP // 2, axis=0), TP // 2, axis=1)
    upstream = jnp.where(pixel_mask[:, :, None] > 0, cotangent, jnp.zeros_like(cotangent))
    upstream = upstream.astype(jnp.float32)[None]
    unused_two, pull_two = jax.vjp(spread_conv, middle.astype(jnp.float32), second)
    mid_raw, grad_two = pull_two(upstream)
    mid_grad = jnp.where(middle > 0, mid_raw, 0.0).astype(jnp.bfloat16)
    unused_one, pull_one = jax.vjp(stride_conv, picture, first)
    picture_grad, grad_one = pull_one(mid_grad.astype(jnp.float32))
    scale = 1.0 / math.sqrt(PIXELS)
    input_grad = picture_grad[0].reshape(SH, SW * CIN).astype(jnp.bfloat16)
    return (input_grad, grad_one * scale, grad_two * scale)
```

```python
import functools
import math

import jax
import jax.numpy as jnp
from jax import lax
from jax.experimental import pallas as pl
from jax.experimental.pallas import tpu as pltpu
from jax.sharding import PartitionSpec as P

TP = 12
TISS_MEAN = 8
BF = jnp.bfloat16
F32 = jnp.float32
SLOTS = 64


def swaps(size, distance):
    return [(i, i ^ distance) for i in range(size) if (i ^ distance) < size]


def odd_swaps(size):
    return [p for i in range(1, size - 1, 2) for p in ((i, i + 1), (i + 1, i))]


def neighbour_strips(first, last, axis):
    size = lax.axis_size(axis)
    even = lax.axis_index(axis) % 2 == 0
    if size == 1:
        return jnp.zeros_like(first), jnp.zeros_like(first)
    got_even = lax.ppermute(jnp.where(even, last, first), axis, swaps(size, 1))
    if size == 2:
        got_odd = jnp.zeros_like(first)
    else:
        got_odd = lax.ppermute(jnp.where(even, first, last), axis, odd_swaps(size))
    return jnp.where(even, got_odd, got_even), jnp.where(even, got_even, got_odd)


def joined_halves(own, axis_dim):
    other = lax.ppermute(own, "chan", [(0, 1), (1, 0)])
    low = lax.axis_index("chan") == 0
    return jnp.concatenate(
        [jnp.where(low, own, other), jnp.where(low, other, own)], axis=axis_dim
    )


def roll_columns(value, amount):
    return pltpu.roll(value, amount % SLOTS, axis=1)


def main_kernel(flags, a_ref, u_ref, wa_ref, w2_ref, shift_ref, grad_ref, weight_ref):
    rows = a_ref.shape[0] - 2
    tall = rows + 1
    own_cols = grad_ref.shape[2]
    lanes = a_ref.shape[3]

    def flat(value):
        return value.reshape(value.shape[0] * SLOTS, value.shape[2])

    def image(value):
        return value.reshape(value.shape[0] // SLOTS, SLOTS, value.shape[1])

    def a_rows(count):
        return jnp.concatenate(
            [
                flat(a_ref[0:count, 1]),
                flat(a_ref[1 : count + 1, 0]),
                flat(a_ref[1 : count + 1, 1]),
            ],
            axis=1,
        )

    def u_rows(count):
        return jnp.concatenate([flat(u_ref[5 - 2 * u : 5 - 2 * u + count]) for u in range(3)], axis=1)

    row_id = lax.broadcasted_iota(jnp.int32, (tall, SLOTS, lanes), 0)
    col_id = lax.broadcasted_iota(jnp.int32, (tall, SLOTS, lanes), 1)
    own = (row_id < rows) & (col_id < own_cols)
    last_row = rows + flags[0]
    last_col = own_cols + flags[1]
    valid = (row_id < last_row) & (col_id < last_col)

    wa = wa_ref[...]
    part = jnp.dot(a_rows(tall), wa, preferred_element_type=F32)
    pre = image(part[:, lanes:]) + roll_columns(image(part[:, :lanes]), 1) + shift_ref[0]
    middle = jnp.maximum(pre, 0.0).astype(BF).astype(F32)

    mid_part = jnp.dot(u_rows(tall), w2_ref[...], preferred_element_type=F32)
    mid_raw = (
        roll_columns(image(mid_part[:, :lanes]), -2)
        + image(mid_part[:, lanes : 2 * lanes])
        + roll_columns(image(mid_part[:, 2 * lanes :]), 2)
    )
    mid_grad = jnp.where((middle > 0) & valid, mid_raw, 0.0)

    middle_own = jnp.where(own, middle, 0.0)[:rows]
    middle_taps = jnp.concatenate(
        [
            flat(roll_columns(middle_own, 2)).astype(BF),
            flat(middle_own).astype(BF),
            flat(roll_columns(middle_own, -2)).astype(BF),
        ],
        axis=1,
    )
    over_pixels = (((0,), (0,)), ((), ()))
    second = lax.dot_general(middle_taps, u_rows(rows), over_pixels, preferred_element_type=F32)

    grad_own = jnp.where(own, mid_grad, 0.0)[:rows]
    grad_taps = jnp.concatenate(
        [flat(roll_columns(grad_own, -1)).astype(BF), flat(grad_own).astype(BF)], axis=1
    )
    first = lax.dot_general(a_rows(rows), grad_taps, over_pixels, preferred_element_type=F32)

    low = flags[2] == 0
    half = lanes // 2
    left = lax.broadcasted_iota(jnp.int32, (48, lanes), 1) < half
    for u in range(3):
        for w in range(3):
            a_row = u * lanes + (0 if w == 1 else half)
            a_col = 0 if w == 0 else lanes
            both = jnp.concatenate(
                [
                    second[w * lanes : (w + 1) * lanes, u * lanes : (u + 1) * lanes],
                    first[a_row : a_row + half, a_col : a_col + lanes],
                ],
                axis=0,
            )
            turned = pltpu.roll(both, half, axis=1)
            at_left = jnp.where(low, both, turned)
            at_right = jnp.where(low, turned, both)
            tap = u * 3 + w
            for h in range(2):
                packed = jnp.where(
                    left, at_left[96 * h : 96 * h + 48], at_right[96 * h + 48 : 96 * h + 96]
                )
                weight_ref[h, tap * 48 : tap * 48 + 48, :] = packed.astype(BF)

    by_lanes = (((1,), (1,)), ((), ()))
    grads = flat(mid_grad).astype(BF)
    straight = lax.dot_general(grads, wa[:, lanes:], by_lanes, preferred_element_type=F32)
    shifted = lax.dot_general(grads, wa[:, :lanes], by_lanes, preferred_element_type=F32)

    def taps(u):
        s = slice(u * lanes, (u + 1) * lanes)
        return image(straight[:, s]) + roll_columns(image(shifted[:, s]), -1)

    above, level, below = taps(0), taps(1), taps(2)
    grad_ref[:, 0] = level[:rows, :own_cols].astype(BF)
    grad_ref[:, 1] = (below[:rows, :own_cols] + above[1:tall, :own_cols]).astype(BF)


def unpack_kernel(scale, flags, own_ref, other_ref, first_ref, second_ref):
    low = flags[0] == 0
    half = first_ref.shape[2]
    for h in range(2):
        here = low if h == 0 else jnp.logical_not(low)
        for tap in range(9):
            rows = slice(tap * 48, tap * 48 + 48)
            value = (
                jnp.where(here, own_ref[rows, :].astype(F32), other_ref[rows, :].astype(F32)) * scale
            )
            for side in range(2):
                part = value[:, side * half : (side + 1) * half]
                start = 96 * h + 48 * side
                to_second = max(0, min(48, 128 - start))
                if to_second > 0:
                    second_ref[tap, start : start + to_second, :] = part[:to_second]
                if to_second < 48:
                    at = start + to_second - 128
                    first_ref[tap, at : at + 48 - to_second, :] = part[to_second:]


def summed_pair(value, axis, size, distance):
    got = lax.ppermute(value, axis, swaps(size, distance))
    return (value.astype(F32) + got.astype(F32)).astype(BF)


def shards(acts, shift, weight_one, weight_two, cotangent, tissue_count, tile_order):
    channels, mids = weight_one.shape[2], weight_one.shape[3]
    height = acts.shape[0]
    lanes = 2 * channels
    pairs = acts.shape[1] // lanes
    rows, cols = height // 2, pairs
    tile_rows, tile_cols = height // TP, 2 * pairs // TP
    out_side = TP // 2
    n_rows, n_tiles = lax.axis_size("rows"), lax.axis_size("tiles")
    row_index, tile_index = lax.axis_index("rows"), lax.axis_index("tiles")
    chan_index = lax.axis_index("chan")

    order = tile_order[0, 0]
    ranks = jnp.arange(order.shape[0], dtype=jnp.int32)
    hits = (order[:, None] == ranks[None, :]) & (ranks[:, None] < tissue_count[0, 0])
    tissue = jnp.sum(hits.astype(jnp.int32), axis=0).reshape(tile_rows, tile_cols)
    pixel_mask = jnp.repeat(jnp.repeat(tissue, out_side, axis=0), out_side, axis=1)
    masked = jnp.where(pixel_mask[:, :, None] > 0, cotangent, jnp.zeros_like(cotangent))
    upstream = joined_halves(masked, 2)
    second_full = joined_halves(weight_two, 3)

    picture = acts.reshape(height, pairs, lanes)
    strip = lambda a, u: jnp.concatenate([a, u], axis=0)
    before, after = neighbour_strips(
        strip(picture[:2], upstream[:3]), strip(picture[height - 2 :], upstream[rows - 3 :]), "rows"
    )
    tall_a = jnp.concatenate([before[:2], picture, after[:2]], axis=0)
    tall_u = jnp.concatenate([before[2:], upstream, after[2:]], axis=0)

    n_a, n_u = tall_a.shape[0], tall_u.shape[0]
    side = lambda a, u: jnp.concatenate([a.reshape(n_a, lanes), u.reshape(4 * n_u, lanes)], axis=0)
    before, after = neighbour_strips(
        side(tall_a[:, :1], tall_u[:, :4]), side(tall_a[:, cols - 1 :], tall_u[:, cols - 4 :]), "tiles"
    )

    def circular(middle, a, b):
        gap = SLOTS - cols - a.shape[1] - b.shape[1]
        fill = jnp.zeros((middle.shape[0], gap, lanes), BF)
        return jnp.concatenate([middle, a, fill, b], axis=1)

    full_a = circular(tall_a, after[:n_a].reshape(n_a, 1, lanes), before[:n_a].reshape(n_a, 1, lanes))
    full_u = circular(
        tall_u, after[n_a:].reshape(n_u, 4, lanes), before[n_a:].reshape(n_u, 4, lanes)
    )

    straight = weight_one[:, 1:].reshape(3, lanes, mids)
    shifted = jnp.concatenate([jnp.zeros_like(weight_one[:, 0]), weight_one[:, 0]], axis=1)
    wa = jnp.concatenate([shifted, straight], axis=2).reshape(3 * lanes, 2 * mids)
    w2 = second_full.transpose(0, 3, 1, 2).reshape(3 * lanes, 3 * mids)
    flags = jnp.stack(
        [
            (row_index < n_rows - 1).astype(jnp.int32),
            (tile_index < n_tiles - 1).astype(jnp.int32),
            chan_index,
        ]
    )
    whole = pl.BlockSpec(memory_space=pltpu.VMEM)
    scalars = pl.BlockSpec(memory_space=pltpu.SMEM)
    limit = pltpu.CompilerParams(vmem_limit_bytes=48 << 20)
    input_grad, weights = pl.pallas_call(
        main_kernel,
        out_shape=(
            jax.ShapeDtypeStruct((rows, 2, cols, lanes), BF),
            jax.ShapeDtypeStruct((2, 9 * 48, lanes), BF),
        ),
        in_specs=[scalars] + [whole] * 5,
        out_specs=(whole, whole),
        compiler_params=limit,
    )(flags, full_a.reshape(rows + 2, 2, SLOTS, lanes), full_u, wa, w2, shift.reshape(1, mids))

    even = row_index % 2 == 0
    if n_rows > 1:
        kept = jnp.where(even, weights[0], weights[1])
        sent = jnp.where(even, weights[1], weights[0])
        got = lax.ppermute(sent, "rows", swaps(n_rows, 1))
        total = (kept.astype(F32) + got.astype(F32)).astype(BF)
    distance = 2
    while distance < n_rows:
        total = summed_pair(total, "rows", n_rows, distance)
        distance *= 2
    if n_tiles == 4:
        one, two, three = (lax.ppermute(total, "tiles", swaps(4, d)) for d in (1, 2, 3))
        total = (
            (total.astype(F32) + one.astype(F32)) + (two.astype(F32) + three.astype(F32))
        ).astype(BF)
    else:
        distance = 1
        while distance < n_tiles:
            total = summed_pair(total, "tiles", n_tiles, distance)
            distance *= 2
    other = lax.ppermute(total, "rows", swaps(n_rows, 1))

    pixels = n_rows * TISS_MEAN * n_tiles * out_side * out_side
    scale = 1.0 / math.sqrt(pixels)
    half = mids // 2
    first, second = pl.pallas_call(
        functools.partial(unpack_kernel, scale),
        out_shape=(
            jax.ShapeDtypeStruct((9, channels, half), F32),
            jax.ShapeDtypeStruct((9, mids, half), F32),
        ),
        in_specs=[scalars, whole, whole],
        out_specs=(whole, whole),
        compiler_params=limit,
    )(row_index.reshape(1) % 2, total, other)
    return (
        input_grad.reshape(height, pairs * lanes),
        first.reshape(3, 3, channels, half),
        second.reshape(3, 3, mids, half),
    )


def solution(mesh):
    return jax.shard_map(
        shards,
        mesh=mesh,
        in_specs=(
            P(("groups", "rows"), "tiles"),
            P(),
            P(),
            P(None, None, None, "chan"),
            P(("groups", "rows"), "tiles", "chan"),
            P(("groups", "rows"), "tiles"),
            P(("groups", "rows"), "tiles", None),
        ),
        out_specs=(
            P(("groups", "rows"), "tiles"),
            P("groups", None, None, "chan"),
            P("groups", None, None, "chan"),
        ),
        check_vma=False,
    )
```

```python
import functools
import math

import jax
import jax.numpy as jnp
from jax import lax
from jax.experimental import pallas as pl
from jax.experimental.pallas import tpu as pltpu
from jax.sharding import PartitionSpec as P

TP = 12
TISS_MEAN = 8
BF = jnp.bfloat16
F32 = jnp.float32
SLOTS = 64


def swaps(size, distance):
    return [(i, i ^ distance) for i in range(size) if (i ^ distance) < size]


def odd_swaps(size):
    return [p for i in range(1, size - 1, 2) for p in ((i, i + 1), (i + 1, i))]


def neighbour_strips(first, last, axis):
    size = lax.axis_size(axis)
    even = lax.axis_index(axis) % 2 == 0
    if size == 1:
        return jnp.zeros_like(first), jnp.zeros_like(first)
    got_even = lax.ppermute(jnp.where(even, last, first), axis, swaps(size, 1))
    if size == 2:
        got_odd = jnp.zeros_like(first)
    else:
        got_odd = lax.ppermute(jnp.where(even, first, last), axis, odd_swaps(size))
    return jnp.where(even, got_odd, got_even), jnp.where(even, got_even, got_odd)


def roll_columns(value, amount):
    return pltpu.roll(value, amount % SLOTS, axis=1)


def prepare_kernel(count, order, chan, cot_hbm, w1_hbm, z_ref, wa_ref, cot, w1, tissue, sems):
    copies = [
        pltpu.make_async_copy(cot_hbm, cot, sems.at[0]),
        pltpu.make_async_copy(w1_hbm, w1, sems.at[1]),
    ]
    for copy in copies:
        copy.start()
    tiles = order.shape[2]
    for k in range(tiles):
        tissue[order[0, 0, k]] = jnp.where(k < count[0, 0], 1, 0)
    rows, cols, half = cot.shape
    side = TP // 2
    across = cols // side
    col_id = lax.broadcasted_iota(jnp.int32, (cols, 2 * half), 0)
    lane_id = lax.broadcasted_iota(jnp.int32, (cols, 2 * half), 1)
    mine = (lane_id < half) == (chan[0] == 0)
    masks = []
    for a in range(rows // side):
        live = jnp.zeros((cols, 2 * half), jnp.int32)
        for b in range(across):
            inside = (col_id >= b * side) & (col_id < (b + 1) * side)
            live = jnp.where(inside, tissue[a * across + b], live)
        masks.append((live > 0) & mine)
    copies[0].wait()
    for i in range(rows):
        value = cot[i].astype(F32)
        twice = jnp.concatenate([value, value], axis=1)
        z_ref[i] = jnp.where(masks[i // side], twice, 0.0).astype(BF)
    copies[1].wait()
    lanes = 2 * half
    for u in range(3):
        low = slice(u * lanes, u * lanes + half)
        high = slice(u * lanes + half, (u + 1) * lanes)
        wa_ref[low, :lanes] = jnp.zeros((half, lanes), BF)
        wa_ref[high, :lanes] = w1[u, 0]
        wa_ref[low, lanes:] = w1[u, 1]
        wa_ref[high, lanes:] = w1[u, 2]


def main_kernel(
    flags, a_ref, u_ref, wa_ref, own_w2, other_w2, shift_ref, grad_ref, weight_ref, w2_ref
):
    rows = a_ref.shape[0] - 2
    tall = rows + 1
    own_cols = grad_ref.shape[2]
    lanes = a_ref.shape[3]
    half = lanes // 2
    low = flags[2] == 0

    def flat(value):
        return value.reshape(value.shape[0] * SLOTS, value.shape[2])

    def image(value):
        return value.reshape(value.shape[0] // SLOTS, SLOTS, value.shape[1])

    def a_rows(count):
        return jnp.concatenate(
            [
                flat(a_ref[0:count, 1]),
                flat(a_ref[1 : count + 1, 0]),
                flat(a_ref[1 : count + 1, 1]),
            ],
            axis=1,
        )

    def u_rows(count):
        return jnp.concatenate([flat(u_ref[5 - 2 * u : 5 - 2 * u + count]) for u in range(3)], axis=1)

    for u in range(3):
        for w in range(3):
            own_w, other_w = own_w2[u, w], other_w2[u, w]
            across = slice(w * lanes, (w + 1) * lanes)
            w2_ref[u * lanes : u * lanes + half, across] = jnp.where(low, own_w, other_w)
            w2_ref[u * lanes + half : (u + 1) * lanes, across] = jnp.where(low, other_w, own_w)

    row_id = lax.broadcasted_iota(jnp.int32, (tall, SLOTS, lanes), 0)
    col_id = lax.broadcasted_iota(jnp.int32, (tall, SLOTS, lanes), 1)
    own = (row_id < rows) & (col_id < own_cols)
    last_row = rows + flags[0]
    last_col = own_cols + flags[1]
    valid = (row_id < last_row) & (col_id < last_col)

    wa = wa_ref[...]
    part = jnp.dot(a_rows(tall), wa, preferred_element_type=F32)
    pre = image(part[:, lanes:]) + roll_columns(image(part[:, :lanes]), 1) + shift_ref[0]
    middle = jnp.maximum(pre, 0.0).astype(BF).astype(F32)

    mid_part = jnp.dot(u_rows(tall), w2_ref[...], preferred_element_type=F32)
    mid_raw = (
        roll_columns(image(mid_part[:, :lanes]), -2)
        + image(mid_part[:, lanes : 2 * lanes])
        + roll_columns(image(mid_part[:, 2 * lanes :]), 2)
    )
    mid_grad = jnp.where((middle > 0) & valid, mid_raw, 0.0)

    middle_own = jnp.where(own, middle, 0.0)[:rows]
    middle_taps = jnp.concatenate(
        [
            flat(roll_columns(middle_own, 2)).astype(BF),
            flat(middle_own).astype(BF),
            flat(roll_columns(middle_own, -2)).astype(BF),
        ],
        axis=1,
    )
    over_pixels = (((0,), (0,)), ((), ()))
    second = lax.dot_general(u_rows(rows), middle_taps, over_pixels, preferred_element_type=F32)

    grad_own = jnp.where(own, mid_grad, 0.0)[:rows]
    grad_taps = jnp.concatenate(
        [flat(roll_columns(grad_own, -1)).astype(BF), flat(grad_own).astype(BF)], axis=1
    )
    first = lax.dot_general(a_rows(rows), grad_taps, over_pixels, preferred_element_type=F32)

    left = lax.broadcasted_iota(jnp.int32, (half, lanes), 1) < half

    def keep(block, value):
        at = block % 7 * half
        weight_ref[block // 7, at : at + half, :] = value.astype(BF)

    def at_left(value):
        return jnp.where(low, value, pltpu.roll(value, half, axis=1))

    def at_right(value):
        return jnp.where(low, pltpu.roll(value, half, axis=1), value)

    centre = []
    for u in range(3):
        top = u * lanes
        for w in range(3):
            across = slice(w * lanes, (w + 1) * lanes)
            keep(
                u * 3 + w,
                jnp.where(low, second[top : top + half, across], second[top + half : top + lanes, across]),
            )
        outer = first[top + half : top + lanes]
        keep(9 + u, jnp.where(left, at_left(outer[:, :lanes]), at_right(outer[:, lanes:])))
        centre.append(first[top : top + half, lanes:])
    keep(12, jnp.where(left, at_left(centre[0]), at_right(centre[1])))
    keep(13, at_left(centre[2]))

    by_lanes = (((1,), (1,)), ((), ()))
    grads = flat(mid_grad).astype(BF)
    straight = lax.dot_general(grads, wa[:, lanes:], by_lanes, preferred_element_type=F32)
    shifted = lax.dot_general(grads, wa[:, :lanes], by_lanes, preferred_element_type=F32)

    def taps(u):
        s = slice(u * lanes, (u + 1) * lanes)
        return image(straight[:, s]) + roll_columns(image(shifted[:, s]), -1)

    above, level, below = taps(0), taps(1), taps(2)
    grad_ref[:, 0] = level[:rows, :own_cols].astype(BF)
    grad_ref[:, 1] = (below[:rows, :own_cols] + above[1:tall, :own_cols]).astype(BF)


def unpack_kernel(scale, flags, own_ref, other_ref, first_ref, second_ref):
    low = flags[0] == 0
    half = first_ref.shape[2]

    def block(number):
        here = low if number < 7 else jnp.logical_not(low)
        rows = slice(number % 7 * half, number % 7 * half + half)
        return jnp.where(here, own_ref[rows, :].astype(F32), other_ref[rows, :].astype(F32)) * scale

    for tap in range(9):
        second_ref[tap] = block(tap)
    for u in range(3):
        value = block(9 + u)
        first_ref[3 * u] = value[:, :half]
        first_ref[3 * u + 2] = value[:, half:]
    value = block(12)
    first_ref[1] = value[:, :half]
    first_ref[4] = value[:, half:]
    first_ref[7] = block(13)[:, :half]


def summed_pair(value, axis, size, distance):
    got = lax.ppermute(value, axis, swaps(size, distance))
    return (value.astype(F32) + got.astype(F32)).astype(BF)


def shards(acts, shift, weight_one, weight_two, cotangent, tissue_count, tile_order):
    channels, mids = weight_one.shape[2], weight_one.shape[3]
    height = acts.shape[0]
    lanes = 2 * channels
    pairs = acts.shape[1] // lanes
    rows, cols = height // 2, pairs
    tile_rows, tile_cols = height // TP, 2 * pairs // TP
    out_side = TP // 2
    n_rows, n_tiles = lax.axis_size("rows"), lax.axis_size("tiles")
    row_index, tile_index = lax.axis_index("rows"), lax.axis_index("tiles")
    chan_index = lax.axis_index("chan")

    whole = pl.BlockSpec(memory_space=pltpu.VMEM)
    scalars = pl.BlockSpec(memory_space=pltpu.SMEM)
    in_place = pl.BlockSpec(memory_space=pl.ANY)
    limit = pltpu.CompilerParams(vmem_limit_bytes=48 << 20)
    half = channels
    placed, wa = pl.pallas_call(
        prepare_kernel,
        out_shape=(
            jax.ShapeDtypeStruct((rows, cols, lanes), BF),
            jax.ShapeDtypeStruct((3 * lanes, 2 * mids), BF),
        ),
        in_specs=[scalars, scalars, scalars, in_place, in_place],
        out_specs=(whole, whole),
        scratch_shapes=[
            pltpu.VMEM((rows, cols, half), BF),
            pltpu.VMEM((3, 3, channels, mids), BF),
            pltpu.SMEM((tile_rows * tile_cols,), jnp.int32),
            pltpu.SemaphoreType.DMA((2,)),
        ],
        compiler_params=limit,
    )(tissue_count, tile_order, chan_index.reshape(1), cotangent, weight_one)
    core_swap = [(0, 1), (1, 0)]
    upstream = placed + lax.ppermute(placed, "chan", core_swap)
    own_w2 = weight_two.swapaxes(2, 3)
    other_w2 = lax.ppermute(own_w2, "chan", core_swap)

    picture = acts.reshape(height, pairs, lanes)
    strip = lambda a, u: jnp.concatenate([a, u], axis=0)
    before, after = neighbour_strips(
        strip(picture[:2], upstream[:3]), strip(picture[height - 2 :], upstream[rows - 3 :]), "rows"
    )
    tall_a = jnp.concatenate([before[:2], picture, after[:2]], axis=0)
    tall_u = jnp.concatenate([before[2:], upstream, after[2:]], axis=0)

    n_a, n_u = tall_a.shape[0], tall_u.shape[0]
    side = lambda a, u: jnp.concatenate([a.reshape(n_a, lanes), u.reshape(4 * n_u, lanes)], axis=0)
    before, after = neighbour_strips(
        side(tall_a[:, :1], tall_u[:, :4]), side(tall_a[:, cols - 1 :], tall_u[:, cols - 4 :]), "tiles"
    )

    def circular(middle, a, b):
        gap = SLOTS - cols - a.shape[1] - b.shape[1]
        fill = jnp.zeros((middle.shape[0], gap, lanes), BF)
        return jnp.concatenate([middle, a, fill, b], axis=1)

    full_a = circular(tall_a, after[:n_a].reshape(n_a, 1, lanes), before[:n_a].reshape(n_a, 1, lanes))
    full_u = circular(
        tall_u, after[n_a:].reshape(n_u, 4, lanes), before[n_a:].reshape(n_u, 4, lanes)
    )

    flags = jnp.stack(
        [
            (row_index < n_rows - 1).astype(jnp.int32),
            (tile_index < n_tiles - 1).astype(jnp.int32),
            chan_index,
        ]
    )
    input_grad, weights = pl.pallas_call(
        main_kernel,
        out_shape=(
            jax.ShapeDtypeStruct((rows, 2, cols, lanes), BF),
            jax.ShapeDtypeStruct((2, 7 * half, lanes), BF),
        ),
        in_specs=[scalars] + [whole] * 6,
        out_specs=(whole, whole),
        scratch_shapes=[pltpu.VMEM((3 * lanes, 3 * mids), BF)],
        compiler_params=limit,
    )(
        flags,
        full_a.reshape(rows + 2, 2, SLOTS, lanes),
        full_u,
        wa,
        own_w2,
        other_w2,
        shift.reshape(1, mids),
    )

    even = row_index % 2 == 0
    if n_rows > 1:
        kept = jnp.where(even, weights[0], weights[1])
        sent = jnp.where(even, weights[1], weights[0])
        got = lax.ppermute(sent, "rows", swaps(n_rows, 1))
        total = (kept.astype(F32) + got.astype(F32)).astype(BF)
    distance = 2
    while distance < n_rows:
        total = summed_pair(total, "rows", n_rows, distance)
        distance *= 2
    if n_tiles == 4:
        one, two, three = (lax.ppermute(total, "tiles", swaps(4, d)) for d in (1, 2, 3))
        total = (
            (total.astype(F32) + one.astype(F32)) + (two.astype(F32) + three.astype(F32))
        ).astype(BF)
    else:
        distance = 1
        while distance < n_tiles:
            total = summed_pair(total, "tiles", n_tiles, distance)
            distance *= 2
    other = lax.ppermute(total, "rows", swaps(n_rows, 1))

    pixels = n_rows * TISS_MEAN * n_tiles * out_side * out_side
    scale = 1.0 / math.sqrt(pixels)
    first, second = pl.pallas_call(
        functools.partial(unpack_kernel, scale),
        out_shape=(
            jax.ShapeDtypeStruct((9, channels, half), F32),
            jax.ShapeDtypeStruct((9, half, mids), F32),
        ),
        in_specs=[scalars, whole, whole],
        out_specs=(whole, whole),
        compiler_params=limit,
    )(row_index.reshape(1) % 2, total, other)
    return (
        input_grad.reshape(height, pairs * lanes),
        first.reshape(3, 3, channels, half),
        second.reshape(3, 3, half, mids).swapaxes(2, 3),
    )


def solution(mesh):
    return jax.shard_map(
        shards,
        mesh=mesh,
        in_specs=(
            P(("groups", "rows"), "tiles"),
            P(),
            P(),
            P(None, None, None, "chan"),
            P(("groups", "rows"), "tiles", "chan"),
            P(("groups", "rows"), "tiles"),
            P(("groups", "rows"), "tiles", None),
        ),
        out_specs=(
            P(("groups", "rows"), "tiles"),
            P("groups", None, None, "chan"),
            P("groups", None, None, "chan"),
        ),
        check_vma=False,
    )
```

```python
import functools
import math

import jax
import jax.numpy as jnp
from jax import lax
from jax.experimental import pallas as pl
from jax.experimental.pallas import tpu as pltpu
from jax.sharding import PartitionSpec as P

TP = 12
TISS_MEAN = 8
BF = jnp.bfloat16
F32 = jnp.float32
SLOTS = 64


def swaps(size, distance):
    return [(i, i ^ distance) for i in range(size) if (i ^ distance) < size]


def odd_swaps(size):
    return [p for i in range(1, size - 1, 2) for p in ((i, i + 1), (i + 1, i))]


def permuted(value, axis, pairs, crossing):
    if not crossing:
        return lax.ppermute(value, axis, pairs)
    both = [(2 * i + c, 2 * j + 1 - c) for i, j in pairs for c in range(2)]
    return lax.ppermute(value, (axis, "chan"), both)


def neighbour_strips(first, last, axis, crossing=False):
    size = lax.axis_size(axis)
    even = lax.axis_index(axis) % 2 == 0
    if size == 1:
        return jnp.zeros_like(first), jnp.zeros_like(first)
    got_even = permuted(jnp.where(even, last, first), axis, swaps(size, 1), crossing)
    if size == 2:
        got_odd = jnp.zeros_like(first)
    else:
        got_odd = permuted(jnp.where(even, first, last), axis, odd_swaps(size), crossing)
    return jnp.where(even, got_odd, got_even), jnp.where(even, got_even, got_odd)


def roll_columns(value, amount):
    return pltpu.roll(value, amount % SLOTS, axis=1)


def prepare_kernel(
    chan,
    count,
    order_hbm,
    cot_hbm,
    w1_hbm,
    w2_hbm,
    shift_hbm,
    z_ref,
    wa_ref,
    w2_ref,
    shift_ref,
    cot,
    w1,
    order,
    tissue,
    sems,
):
    pairs = [
        (order_hbm, order),
        (cot_hbm, cot),
        (w1_hbm, w1),
        (w2_hbm, w2_ref),
        (shift_hbm, shift_ref),
    ]
    copies = [pltpu.make_async_copy(a, b, sems.at[i]) for i, (a, b) in enumerate(pairs)]
    for copy in copies:
        copy.start()
    copies[0].wait()
    tiles = order.shape[2]
    for k in range(tiles):
        tissue[order[0, 0, k]] = jnp.where(k < count[0, 0], 1, 0)
    rows, cols, half = cot.shape
    side = TP // 2
    across = cols // side
    col_id = lax.broadcasted_iota(jnp.int32, (cols, 2 * half), 0)
    lane_id = lax.broadcasted_iota(jnp.int32, (cols, 2 * half), 1)
    mine = (lane_id < half) == (chan[0] == 0)
    masks = []
    for a in range(rows // side):
        live = jnp.zeros((cols, 2 * half), jnp.int32)
        for b in range(across):
            inside = (col_id >= b * side) & (col_id < (b + 1) * side)
            live = jnp.where(inside, tissue[a * across + b], live)
        masks.append((live > 0) & mine)
    copies[1].wait()
    for i in range(rows):
        value = cot[i].astype(F32)
        twice = jnp.concatenate([value, value], axis=1)
        z_ref[i] = jnp.where(masks[i // side], twice, 0.0).astype(BF)
    copies[2].wait()
    lanes = 2 * half
    for u in range(3):
        low = slice(u * lanes, u * lanes + half)
        high = slice(u * lanes + half, (u + 1) * lanes)
        wa_ref[low, :lanes] = jnp.zeros((half, lanes), BF)
        wa_ref[high, :lanes] = w1[u, 0]
        wa_ref[low, lanes:] = w1[u, 1]
        wa_ref[high, lanes:] = w1[u, 2]
    copies[3].wait()
    copies[4].wait()


def main_kernel(
    flags, a_ref, u_ref, wa_ref, own_w2, other_w2, shift_ref, grad_ref, weight_ref, w2_ref
):
    rows = a_ref.shape[0] - 2
    tall = rows + 1
    own_cols = grad_ref.shape[2]
    lanes = a_ref.shape[3]
    half = lanes // 2
    low = flags[2] == 0

    def flat(value):
        return value.reshape(value.shape[0] * SLOTS, value.shape[2])

    def image(value):
        return value.reshape(value.shape[0] // SLOTS, SLOTS, value.shape[1])

    def a_rows(count):
        return jnp.concatenate(
            [
                flat(a_ref[0:count, 1]),
                flat(a_ref[1 : count + 1, 0]),
                flat(a_ref[1 : count + 1, 1]),
            ],
            axis=1,
        )

    def u_rows(count):
        return jnp.concatenate([flat(u_ref[5 - 2 * u : 5 - 2 * u + count]) for u in range(3)], axis=1)

    for u in range(3):
        for w in range(3):
            own_w, other_w = own_w2[u, w], other_w2[u, w]
            across = slice(w * lanes, (w + 1) * lanes)
            w2_ref[u * lanes : u * lanes + half, across] = jnp.where(low, own_w, other_w)
            w2_ref[u * lanes + half : (u + 1) * lanes, across] = jnp.where(low, other_w, own_w)

    row_id = lax.broadcasted_iota(jnp.int32, (tall, SLOTS, lanes), 0)
    col_id = lax.broadcasted_iota(jnp.int32, (tall, SLOTS, lanes), 1)
    own = (row_id < rows) & (col_id < own_cols)
    last_row = rows + flags[0]
    last_col = own_cols + flags[1]
    valid = (row_id < last_row) & (col_id < last_col)

    wa = wa_ref[...]
    part = jnp.dot(a_rows(tall), wa, preferred_element_type=F32)
    pre = image(part[:, lanes:]) + roll_columns(image(part[:, :lanes]), 1) + shift_ref[0]
    middle = jnp.maximum(pre, 0.0).astype(BF).astype(F32)

    mid_part = jnp.dot(u_rows(tall), w2_ref[...], preferred_element_type=F32)
    mid_raw = (
        roll_columns(image(mid_part[:, :lanes]), -2)
        + image(mid_part[:, lanes : 2 * lanes])
        + roll_columns(image(mid_part[:, 2 * lanes :]), 2)
    )
    mid_grad = jnp.where((middle > 0) & valid, mid_raw, 0.0)

    middle_own = jnp.where(own, middle, 0.0)[:rows]
    middle_taps = jnp.concatenate(
        [
            flat(roll_columns(middle_own, 2)).astype(BF),
            flat(middle_own).astype(BF),
            flat(roll_columns(middle_own, -2)).astype(BF),
        ],
        axis=1,
    )
    over_pixels = (((0,), (0,)), ((), ()))
    second = lax.dot_general(u_rows(rows), middle_taps, over_pixels, preferred_element_type=F32)

    grad_own = jnp.where(own, mid_grad, 0.0)[:rows]
    grad_taps = jnp.concatenate(
        [flat(roll_columns(grad_own, -1)).astype(BF), flat(grad_own).astype(BF)], axis=1
    )
    first = lax.dot_general(a_rows(rows), grad_taps, over_pixels, preferred_element_type=F32)

    left = lax.broadcasted_iota(jnp.int32, (half, lanes), 1) < half

    def keep(block, value):
        at = block % 7 * half
        weight_ref[block // 7, at : at + half, :] = value.astype(BF)

    def at_left(value):
        return jnp.where(low, value, pltpu.roll(value, half, axis=1))

    def at_right(value):
        return jnp.where(low, pltpu.roll(value, half, axis=1), value)

    centre = []
    for u in range(3):
        top = u * lanes
        for w in range(3):
            across = slice(w * lanes, (w + 1) * lanes)
            keep(
                u * 3 + w,
                jnp.where(low, second[top : top + half, across], second[top + half : top + lanes, across]),
            )
        outer = first[top + half : top + lanes]
        keep(9 + u, jnp.where(left, at_left(outer[:, :lanes]), at_right(outer[:, lanes:])))
        centre.append(first[top : top + half, lanes:])
    keep(12, jnp.where(left, at_left(centre[0]), at_right(centre[1])))
    keep(13, at_left(centre[2]))

    by_lanes = (((1,), (1,)), ((), ()))
    grads = flat(mid_grad).astype(BF)
    straight = lax.dot_general(grads, wa[:, lanes:], by_lanes, preferred_element_type=F32)
    shifted = lax.dot_general(grads, wa[:, :lanes], by_lanes, preferred_element_type=F32)

    def taps(u):
        s = slice(u * lanes, (u + 1) * lanes)
        return image(straight[:, s]) + roll_columns(image(shifted[:, s]), -1)

    above, level, below = taps(0), taps(1), taps(2)
    grad_ref[:, 0] = level[:rows, :own_cols].astype(BF)
    grad_ref[:, 1] = (below[:rows, :own_cols] + above[1:tall, :own_cols]).astype(BF)


def unpack_kernel(scale, flags, own_ref, other_ref, first_ref, second_ref):
    low = flags[0] == 0
    half = first_ref.shape[2]

    def block(number):
        here = low if number < 7 else jnp.logical_not(low)
        rows = slice(number % 7 * half, number % 7 * half + half)
        return jnp.where(here, own_ref[rows, :].astype(F32), other_ref[rows, :].astype(F32)) * scale

    for tap in range(9):
        second_ref[tap] = block(tap)
    for u in range(3):
        value = block(9 + u)
        first_ref[3 * u] = value[:, :half]
        first_ref[3 * u + 2] = value[:, half:]
    value = block(12)
    first_ref[1] = value[:, :half]
    first_ref[4] = value[:, half:]
    first_ref[7] = block(13)[:, :half]


def summed_pair(value, axis, size, distance):
    got = lax.ppermute(value, axis, swaps(size, distance))
    return (value.astype(F32) + got.astype(F32)).astype(BF)


def shards(acts, shift, weight_one, weight_two, cotangent, tissue_count, tile_order):
    channels, mids = weight_one.shape[2], weight_one.shape[3]
    height = acts.shape[0]
    lanes = 2 * channels
    pairs = acts.shape[1] // lanes
    rows, cols = height // 2, pairs
    tile_rows, tile_cols = height // TP, 2 * pairs // TP
    out_side = TP // 2
    n_rows, n_tiles = lax.axis_size("rows"), lax.axis_size("tiles")
    row_index, tile_index = lax.axis_index("rows"), lax.axis_index("tiles")
    chan_index = lax.axis_index("chan")

    whole = pl.BlockSpec(memory_space=pltpu.VMEM)
    scalars = pl.BlockSpec(memory_space=pltpu.SMEM)
    in_hbm = pl.BlockSpec(memory_space=pltpu.HBM)
    limit = pltpu.CompilerParams(vmem_limit_bytes=48 << 20)
    half = channels
    placed, wa, own_w2, shift_row = pl.pallas_call(
        prepare_kernel,
        out_shape=(
            jax.ShapeDtypeStruct((rows, cols, lanes), BF),
            jax.ShapeDtypeStruct((3 * lanes, 2 * mids), BF),
            jax.ShapeDtypeStruct((3, 3, half, mids), BF),
            jax.ShapeDtypeStruct((1, mids), F32),
        ),
        in_specs=[scalars] * 2 + [in_hbm] * 5,
        out_specs=(whole,) * 4,
        scratch_shapes=[
            pltpu.VMEM((rows, cols, half), BF),
            pltpu.VMEM((3, 3, channels, mids), BF),
            pltpu.SMEM((1, 1, tile_rows * tile_cols), jnp.int32),
            pltpu.SMEM((tile_rows * tile_cols,), jnp.int32),
            pltpu.SemaphoreType.DMA((5,)),
        ],
        compiler_params=limit,
    )(
        chan_index.reshape(1),
        tissue_count,
        *(
            pltpu.with_memory_space_constraint(value, pltpu.HBM)
            for value in (
                tile_order,
                cotangent,
                weight_one,
                weight_two.swapaxes(2, 3),
                shift.reshape(1, mids),
            )
        ),
    )

    picture = acts.reshape(height, pairs, lanes)
    strip = lambda a, u: jnp.concatenate([a, u], axis=0)
    before, after = neighbour_strips(
        strip(picture[:2], placed[:3]), strip(picture[height - 2 :], placed[rows - 3 :]), "rows"
    )
    before_x, after_x = neighbour_strips(placed[:3], placed[rows - 3 :], "rows", crossing=True)
    core_swap = [(0, 1), (1, 0)]
    upstream = placed + lax.ppermute(placed, "chan", core_swap)
    other_w2 = lax.ppermute(own_w2, "chan", core_swap)
    tall_a = jnp.concatenate([before[:2], picture, after[:2]], axis=0)
    tall_u = jnp.concatenate([before[2:] + before_x, upstream, after[2:] + after_x], axis=0)

    n_a, n_u = tall_a.shape[0], tall_u.shape[0]
    side = lambda a, u: jnp.concatenate([a.reshape(n_a, lanes), u.reshape(4 * n_u, lanes)], axis=0)
    before, after = neighbour_strips(
        side(tall_a[:, :1], tall_u[:, :4]), side(tall_a[:, cols - 1 :], tall_u[:, cols - 4 :]), "tiles"
    )

    def circular(middle, a, b):
        gap = SLOTS - cols - a.shape[1] - b.shape[1]
        fill = jnp.zeros((middle.shape[0], gap, lanes), BF)
        return jnp.concatenate([middle, a, fill, b], axis=1)

    full_a = circular(tall_a, after[:n_a].reshape(n_a, 1, lanes), before[:n_a].reshape(n_a, 1, lanes))
    full_u = circular(
        tall_u, after[n_a:].reshape(n_u, 4, lanes), before[n_a:].reshape(n_u, 4, lanes)
    )

    flags = jnp.stack(
        [
            (row_index < n_rows - 1).astype(jnp.int32),
            (tile_index < n_tiles - 1).astype(jnp.int32),
            chan_index,
        ]
    )
    input_grad, weights = pl.pallas_call(
        main_kernel,
        out_shape=(
            jax.ShapeDtypeStruct((rows, 2, cols, lanes), BF),
            jax.ShapeDtypeStruct((2, 7 * half, lanes), BF),
        ),
        in_specs=[scalars] + [whole] * 6,
        out_specs=(whole, whole),
        scratch_shapes=[pltpu.VMEM((3 * lanes, 3 * mids), BF)],
        compiler_params=limit,
    )(
        flags,
        full_a.reshape(rows + 2, 2, SLOTS, lanes),
        full_u,
        wa,
        own_w2,
        other_w2,
        shift_row,
    )

    even = row_index % 2 == 0
    if n_rows > 1:
        kept = jnp.where(even, weights[0], weights[1])
        sent = jnp.where(even, weights[1], weights[0])
        got = lax.ppermute(sent, "rows", swaps(n_rows, 1))
        total = (kept.astype(F32) + got.astype(F32)).astype(BF)
    distance = 2
    while distance < n_rows:
        total = summed_pair(total, "rows", n_rows, distance)
        distance *= 2
    if n_tiles == 4:
        one, two, three = (lax.ppermute(total, "tiles", swaps(4, d)) for d in (1, 2, 3))
        total = (
            (total.astype(F32) + one.astype(F32)) + (two.astype(F32) + three.astype(F32))
        ).astype(BF)
    else:
        distance = 1
        while distance < n_tiles:
            total = summed_pair(total, "tiles", n_tiles, distance)
            distance *= 2
    other = lax.ppermute(total, "rows", swaps(n_rows, 1))

    pixels = n_rows * TISS_MEAN * n_tiles * out_side * out_side
    scale = 1.0 / math.sqrt(pixels)
    first, second = pl.pallas_call(
        functools.partial(unpack_kernel, scale),
        out_shape=(
            jax.ShapeDtypeStruct((9, channels, half), F32),
            jax.ShapeDtypeStruct((9, half, mids), F32),
        ),
        in_specs=[scalars, whole, whole],
        out_specs=(whole, whole),
        compiler_params=limit,
    )(row_index.reshape(1) % 2, total, other)
    return (
        input_grad.reshape(height, pairs * lanes),
        first.reshape(3, 3, channels, half),
        second.reshape(3, 3, half, mids).swapaxes(2, 3),
    )


def solution(mesh):
    return jax.shard_map(
        shards,
        mesh=mesh,
        in_specs=(
            P(("groups", "rows"), "tiles"),
            P(),
            P(),
            P(None, None, None, "chan"),
            P(("groups", "rows"), "tiles", "chan"),
            P(("groups", "rows"), "tiles"),
            P(("groups", "rows"), "tiles", None),
        ),
        out_specs=(
            P(("groups", "rows"), "tiles"),
            P("groups", None, None, "chan"),
            P("groups", None, None, "chan"),
        ),
        check_vma=False,
    )
```

```python
import functools
import math

import jax
import jax.numpy as jnp
from jax import lax
from jax.experimental import pallas as pl
from jax.experimental.pallas import tpu as pltpu
from jax.sharding import PartitionSpec as P

TP = 12
TISS_MEAN = 8
BF = jnp.bfloat16
F32 = jnp.float32
SLOTS = 64


def swaps(size, distance):
    return [(i, i ^ distance) for i in range(size) if (i ^ distance) < size]


def core_swapped(value):
    return lax.ppermute(value, "chan", [(0, 1), (1, 0)])


def shared_pairs(axis, n_tiles, n_rows):
    sizes = (n_tiles, n_rows)
    along = ("tiles", "rows").index(axis)
    size = sizes[along]
    pairs = []
    for t in range(n_tiles):
        for r in range(n_rows):
            for core in range(2):
                place, partner = [t, r], [t, r]
                if core == 0:
                    partner[along] = place[along] ^ 1
                else:
                    partner[along] = ((place[along] + 1) ^ 1) - 1
                if not 0 <= partner[along] < size:
                    partner[along] = place[along]
                    partner[1 - along] = place[1 - along] ^ 1
                    if partner[1 - along] >= sizes[1 - along]:
                        continue
                code = lambda p: (p[0] * n_rows + p[1]) * 2 + core
                pairs.append((code(place), code(partner)))
    return pairs


def neighbour_strips(first, last, axis):
    size, index = lax.axis_size(axis), lax.axis_index(axis)
    even = index % 2 == 0
    none = jnp.zeros_like(first)
    if size == 1:
        return none, none
    to_even, to_odd = jnp.where(even, last, first), jnp.where(even, first, last)
    if size == 2:
        got = lax.ppermute(to_even, axis, swaps(size, 1))
        return jnp.where(even, none, got), jnp.where(even, got, none)
    low = lax.axis_index("chan") == 0
    pairs = shared_pairs(axis, lax.axis_size("tiles"), lax.axis_size("rows"))
    got = lax.ppermute(jnp.where(low, to_even, to_odd), ("tiles", "rows", "chan"), pairs)
    other = core_swapped(got)
    own_first = low == even
    before = jnp.where(index == 0, none, jnp.where(own_first, other, got))
    after = jnp.where(index == size - 1, none, jnp.where(own_first, got, other))
    return before, after


def roll_columns(value, amount):
    return pltpu.roll(value, amount % SLOTS, axis=1)


def prepare_kernel(
    chan,
    count,
    order_hbm,
    cot_hbm,
    w1_hbm,
    w2_hbm,
    shift_hbm,
    z_ref,
    wa_ref,
    w2_ref,
    shift_ref,
    cot,
    w1,
    order,
    tissue,
    sems,
):
    pairs = [
        (order_hbm, order),
        (cot_hbm, cot),
        (w1_hbm, w1),
        (w2_hbm, w2_ref),
        (shift_hbm, shift_ref),
    ]
    copies = [pltpu.make_async_copy(a, b, sems.at[i]) for i, (a, b) in enumerate(pairs)]
    for copy in copies:
        copy.start()
    copies[0].wait()
    tiles = order.shape[2]
    for k in range(tiles):
        tissue[order[0, 0, k]] = jnp.where(k < count[0, 0], 1, 0)
    rows, cols, half = cot.shape
    side = TP // 2
    across = cols // side
    col_id = lax.broadcasted_iota(jnp.int32, (cols, 2 * half), 0)
    lane_id = lax.broadcasted_iota(jnp.int32, (cols, 2 * half), 1)
    mine = (lane_id < half) == (chan[0] == 0)
    masks = []
    for a in range(rows // side):
        live = jnp.zeros((cols, 2 * half), jnp.int32)
        for b in range(across):
            inside = (col_id >= b * side) & (col_id < (b + 1) * side)
            live = jnp.where(inside, tissue[a * across + b], live)
        masks.append((live > 0) & mine)
    copies[1].wait()
    for i in range(rows):
        value = cot[i].astype(F32)
        twice = jnp.concatenate([value, value], axis=1)
        z_ref[i] = jnp.where(masks[i // side], twice, 0.0).astype(BF)
    copies[2].wait()
    lanes = 2 * half
    for u in range(3):
        low = slice(u * lanes, u * lanes + half)
        high = slice(u * lanes + half, (u + 1) * lanes)
        wa_ref[low, :lanes] = jnp.zeros((half, lanes), BF)
        wa_ref[high, :lanes] = w1[u, 0]
        wa_ref[low, lanes:] = w1[u, 1]
        wa_ref[high, lanes:] = w1[u, 2]
    copies[3].wait()
    copies[4].wait()


def flat(value):
    return value.reshape(value.shape[0] * SLOTS, value.shape[2])


def image(value):
    return value.reshape(value.shape[0] // SLOTS, SLOTS, value.shape[1])


def main_kernel(
    flags, a_ref, u_ref, wa_ref, own_w2, other_w2, shift_ref, mid_ref, weight_ref, w2_ref
):
    rows = a_ref.shape[0] - 2
    tall = rows + 1
    own_cols = flags[4]
    lanes = a_ref.shape[3]
    half = lanes // 2
    low = flags[2] == 0

    def a_rows(count):
        return jnp.concatenate(
            [
                flat(a_ref[0:count, 1]),
                flat(a_ref[1 : count + 1, 0]),
                flat(a_ref[1 : count + 1, 1]),
            ],
            axis=1,
        )

    def u_rows(count):
        return jnp.concatenate([flat(u_ref[5 - 2 * u : 5 - 2 * u + count]) for u in range(3)], axis=1)

    for u in range(3):
        for w in range(3):
            own_w, other_w = own_w2[u, w], other_w2[u, w]
            across = slice(w * lanes, (w + 1) * lanes)
            w2_ref[u * lanes : u * lanes + half, across] = jnp.where(low, own_w, other_w)
            w2_ref[u * lanes + half : (u + 1) * lanes, across] = jnp.where(low, other_w, own_w)

    row_id = lax.broadcasted_iota(jnp.int32, (tall, SLOTS, lanes), 0)
    col_id = lax.broadcasted_iota(jnp.int32, (tall, SLOTS, lanes), 1)
    own = (row_id < rows) & (col_id < own_cols)
    last_row = rows + flags[0]
    last_col = own_cols + flags[1]
    valid = (row_id < last_row) & (col_id < last_col)

    wa = wa_ref[...]
    part = jnp.dot(a_rows(tall), wa, preferred_element_type=F32)
    pre = image(part[:, lanes:]) + roll_columns(image(part[:, :lanes]), 1) + shift_ref[0]
    middle = jnp.maximum(pre, 0.0).astype(BF).astype(F32)

    mid_part = jnp.dot(u_rows(tall), w2_ref[...], preferred_element_type=F32)
    mid_raw = (
        roll_columns(image(mid_part[:, :lanes]), -2)
        + image(mid_part[:, lanes : 2 * lanes])
        + roll_columns(image(mid_part[:, 2 * lanes :]), 2)
    )
    mid_grad = jnp.where((middle > 0) & valid, mid_raw, 0.0)
    mid_ref[...] = mid_grad.astype(BF)

    middle_own = jnp.where(own, middle, 0.0)[:rows]
    middle_taps = jnp.concatenate(
        [
            flat(roll_columns(middle_own, 2)).astype(BF),
            flat(middle_own).astype(BF),
            flat(roll_columns(middle_own, -2)).astype(BF),
        ],
        axis=1,
    )
    over_pixels = (((0,), (0,)), ((), ()))
    second = lax.dot_general(u_rows(rows), middle_taps, over_pixels, preferred_element_type=F32)

    grad_own = jnp.where(own, mid_grad, 0.0)[:rows]
    grad_taps = jnp.concatenate(
        [flat(roll_columns(grad_own, -1)).astype(BF), flat(grad_own).astype(BF)], axis=1
    )
    first = lax.dot_general(a_rows(rows), grad_taps, over_pixels, preferred_element_type=F32)

    left = lax.broadcasted_iota(jnp.int32, (half, lanes), 1) < half

    part = weight_ref.shape[1]
    me = flags[3]

    def keep(block, value):
        done = 0
        while done < half:
            number, at = divmod(block * half + done, part)
            count = min(part - at, half - done)
            weight_ref[number ^ me, at : at + count, :] = value[done : done + count].astype(BF)
            done += count

    def at_left(value):
        return jnp.where(low, value, pltpu.roll(value, half, axis=1))

    def at_right(value):
        return jnp.where(low, pltpu.roll(value, half, axis=1), value)

    centre = []
    for u in range(3):
        top = u * lanes
        for w in range(3):
            across = slice(w * lanes, (w + 1) * lanes)
            keep(
                u * 3 + w,
                jnp.where(low, second[top : top + half, across], second[top + half : top + lanes, across]),
            )
        outer = first[top + half : top + lanes]
        keep(9 + u, jnp.where(left, at_left(outer[:, :lanes]), at_right(outer[:, lanes:])))
        centre.append(first[top : top + half, lanes:])
    keep(12, jnp.where(left, at_left(centre[0]), at_right(centre[1])))
    keep(13, at_left(centre[2]))


def input_kernel(mid_ref, wa_ref, grad_ref):
    rows, own_cols, lanes = grad_ref.shape[0], grad_ref.shape[2], grad_ref.shape[3]
    tall = rows + 1
    by_lanes = (((1,), (1,)), ((), ()))
    grads = flat(mid_ref[...])
    wa = wa_ref[...]
    straight = lax.dot_general(grads, wa[:, lanes:], by_lanes, preferred_element_type=F32)
    shifted = lax.dot_general(grads, wa[:, :lanes], by_lanes, preferred_element_type=F32)

    def taps(u):
        s = slice(u * lanes, (u + 1) * lanes)
        return image(straight[:, s]) + roll_columns(image(shifted[:, s]), -1)

    above, level, below = taps(0), taps(1), taps(2)
    grad_ref[:, 0] = level[:rows, :own_cols].astype(BF)
    grad_ref[:, 1] = (below[:rows, :own_cols] + above[1:tall, :own_cols]).astype(BF)


def unpack_kernel(scale, flags, piece_0, piece_1, piece_2, piece_3, first_ref, second_ref, all_ref):
    half = first_ref.shape[2]
    part = piece_0.shape[0]
    for distance, piece in enumerate((piece_0, piece_1, piece_2, piece_3)):
        all_ref[flags[0] ^ distance] = piece[...]

    def block(number):
        done, values = 0, []
        while done < half:
            which, at = divmod(number * half + done, part)
            count = min(part - at, half - done)
            values.append(all_ref[which, at : at + count, :].astype(F32) * scale)
            done += count
        return values[0] if len(values) == 1 else jnp.concatenate(values, axis=0)

    for tap in range(9):
        second_ref[tap] = block(tap)
    for u in range(3):
        value = block(9 + u)
        first_ref[3 * u] = value[:, :half]
        first_ref[3 * u + 2] = value[:, half:]
    value = block(12)
    first_ref[1] = value[:, :half]
    first_ref[4] = value[:, half:]
    first_ref[7] = block(13)[:, :half]


def summed_pair(value, axis, size, distance):
    got = lax.ppermute(value, axis, swaps(size, distance))
    return (value.astype(F32) + got.astype(F32)).astype(BF)


def shards(acts, shift, weight_one, weight_two, cotangent, tissue_count, tile_order):
    channels, mids = weight_one.shape[2], weight_one.shape[3]
    height = acts.shape[0]
    lanes = 2 * channels
    pairs = acts.shape[1] // lanes
    rows, cols = height // 2, pairs
    tile_rows, tile_cols = height // TP, 2 * pairs // TP
    out_side = TP // 2
    n_rows, n_tiles = lax.axis_size("rows"), lax.axis_size("tiles")
    row_index, tile_index = lax.axis_index("rows"), lax.axis_index("tiles")
    chan_index = lax.axis_index("chan")

    whole = pl.BlockSpec(memory_space=pltpu.VMEM)
    scalars = pl.BlockSpec(memory_space=pltpu.SMEM)
    in_hbm = pl.BlockSpec(memory_space=pltpu.HBM)
    limit = pltpu.CompilerParams(vmem_limit_bytes=48 << 20)
    half = channels
    placed, wa, own_w2, shift_row = pl.pallas_call(
        prepare_kernel,
        out_shape=(
            jax.ShapeDtypeStruct((rows, cols, lanes), BF),
            jax.ShapeDtypeStruct((3 * lanes, 2 * mids), BF),
            jax.ShapeDtypeStruct((3, 3, half, mids), BF),
            jax.ShapeDtypeStruct((1, mids), F32),
        ),
        in_specs=[scalars] * 2 + [in_hbm] * 5,
        out_specs=(whole,) * 4,
        scratch_shapes=[
            pltpu.VMEM((rows, cols, half), BF),
            pltpu.VMEM((3, 3, channels, mids), BF),
            pltpu.SMEM((1, 1, tile_rows * tile_cols), jnp.int32),
            pltpu.SMEM((tile_rows * tile_cols,), jnp.int32),
            pltpu.SemaphoreType.DMA((5,)),
        ],
        compiler_params=limit,
    )(
        chan_index.reshape(1),
        tissue_count,
        *(
            pltpu.with_memory_space_constraint(value, pltpu.HBM)
            for value in (
                tile_order,
                cotangent,
                weight_one,
                weight_two.swapaxes(2, 3),
                shift.reshape(1, mids),
            )
        ),
    )

    picture = acts.reshape(height, pairs, lanes)
    edges = jnp.stack([placed[:3], placed[rows - 3 :]])
    if n_rows == 2:
        edge = jnp.where(row_index == 0, edges[1], edges[0])
        edge = edge + core_swapped(edge)
        first_u, last_u = edge, edge
    else:
        edges = edges + core_swapped(edges)
        first_u, last_u = edges[0], edges[1]
    strip = lambda a, u: jnp.concatenate([a, u], axis=0)
    before, after = neighbour_strips(
        strip(picture[:2], first_u), strip(picture[height - 2 :], last_u), "rows"
    )
    upstream = placed + core_swapped(placed)
    other_w2 = core_swapped(own_w2)
    tall_a = jnp.concatenate([before[:2], picture, after[:2]], axis=0)
    tall_u = jnp.concatenate([before[2:], upstream, after[2:]], axis=0)

    n_a, n_u = tall_a.shape[0], tall_u.shape[0]
    side = lambda a, u: jnp.concatenate([a.reshape(n_a, lanes), u.reshape(4 * n_u, lanes)], axis=0)
    before, after = neighbour_strips(
        side(tall_a[:, :1], tall_u[:, :4]), side(tall_a[:, cols - 1 :], tall_u[:, cols - 4 :]), "tiles"
    )

    def circular(middle, a, b):
        gap = SLOTS - cols - a.shape[1] - b.shape[1]
        fill = jnp.zeros((middle.shape[0], gap, lanes), BF)
        return jnp.concatenate([middle, a, fill, b], axis=1)

    full_a = circular(tall_a, after[:n_a].reshape(n_a, 1, lanes), before[:n_a].reshape(n_a, 1, lanes))
    full_u = circular(
        tall_u, after[n_a:].reshape(n_u, 4, lanes), before[n_a:].reshape(n_u, 4, lanes)
    )

    quarter = tile_index % 2 * 2 + row_index % 2
    flags = jnp.stack(
        [
            (row_index < n_rows - 1).astype(jnp.int32),
            (tile_index < n_tiles - 1).astype(jnp.int32),
            chan_index,
            quarter,
            jnp.int32(cols),
        ]
    )
    part = 14 * half // 4
    mid_grad, weights = pl.pallas_call(
        main_kernel,
        out_shape=(
            jax.ShapeDtypeStruct((rows + 1, SLOTS, lanes), BF),
            jax.ShapeDtypeStruct((4, part, lanes), BF),
        ),
        in_specs=[scalars] + [whole] * 6,
        out_specs=(whole, whole),
        scratch_shapes=[pltpu.VMEM((3 * lanes, 3 * mids), BF)],
        compiler_params=limit,
    )(
        flags,
        full_a.reshape(rows + 2, 2, SLOTS, lanes),
        full_u,
        wa,
        own_w2,
        other_w2,
        shift_row,
    )
    input_grad = pl.pallas_call(
        input_kernel,
        out_shape=jax.ShapeDtypeStruct((rows, 2, cols, lanes), BF),
        in_specs=[whole, whole],
        out_specs=whole,
        compiler_params=limit,
    )(mid_grad, wa)

    def from_block(values):
        return [
            lax.ppermute(
                value,
                ("tiles", "rows"),
                [
                    (t * n_rows + r, (t ^ (d >> 1)) * n_rows + (r ^ (d & 1)))
                    for t in range(n_tiles)
                    for r in range(n_rows)
                ],
            )
            for d, value in enumerate(values, 1)
        ]

    one, two, three = from_block([weights[1], weights[2], weights[3]])
    total = (
        (weights[0].astype(F32) + one.astype(F32)) + (two.astype(F32) + three.astype(F32))
    ).astype(BF)
    distance = 2
    while distance < n_rows:
        total = summed_pair(total, "rows", n_rows, distance)
        distance *= 2
    distance = 2
    while distance < n_tiles:
        total = summed_pair(total, "tiles", n_tiles, distance)
        distance *= 2
    pieces = [total] + from_block([total] * 3)

    pixels = n_rows * TISS_MEAN * n_tiles * out_side * out_side
    scale = 1.0 / math.sqrt(pixels)
    first, second = pl.pallas_call(
        functools.partial(unpack_kernel, scale),
        out_shape=(
            jax.ShapeDtypeStruct((9, channels, half), F32),
            jax.ShapeDtypeStruct((9, half, mids), F32),
        ),
        in_specs=[scalars] + [whole] * 4,
        out_specs=(whole, whole),
        scratch_shapes=[pltpu.VMEM((4, part, lanes), BF)],
        compiler_params=limit,
    )(quarter.reshape(1), *pieces)
    return (
        input_grad.reshape(height, pairs * lanes),
        first.reshape(3, 3, channels, half),
        second.reshape(3, 3, half, mids).swapaxes(2, 3),
    )


def solution(mesh):
    return jax.shard_map(
        shards,
        mesh=mesh,
        in_specs=(
            P(("groups", "rows"), "tiles"),
            P(),
            P(),
            P(None, None, None, "chan"),
            P(("groups", "rows"), "tiles", "chan"),
            P(("groups", "rows"), "tiles"),
            P(("groups", "rows"), "tiles", None),
        ),
        out_specs=(
            P(("groups", "rows"), "tiles"),
            P("groups", None, None, "chan"),
            P("groups", None, None, "chan"),
        ),
        check_vma=False,
    )
```

```python
import functools
import math

import jax
import jax.numpy as jnp
from jax import lax
from jax.experimental import pallas as pl
from jax.experimental.pallas import tpu as pltpu
from jax.sharding import PartitionSpec as P

TP = 12
TISS_MEAN = 8
BF = jnp.bfloat16
F32 = jnp.float32
SLOTS = 64


def swaps(size, distance):
    return [(i, i ^ distance) for i in range(size) if (i ^ distance) < size]


def core_swapped(value):
    return lax.ppermute(value, "chan", [(0, 1), (1, 0)])


def shared_pairs(axis, n_tiles, n_rows):
    sizes = (n_tiles, n_rows)
    along = ("tiles", "rows").index(axis)
    size = sizes[along]
    pairs = []
    for t in range(n_tiles):
        for r in range(n_rows):
            for core in range(2):
                place, partner = [t, r], [t, r]
                if core == 0:
                    partner[along] = place[along] ^ 1
                else:
                    partner[along] = ((place[along] + 1) ^ 1) - 1
                if not 0 <= partner[along] < size:
                    partner[along] = place[along]
                    partner[1 - along] = place[1 - along] ^ 1
                    if partner[1 - along] >= sizes[1 - along]:
                        continue
                code = lambda p: (p[0] * n_rows + p[1]) * 2 + core
                pairs.append((code(place), code(partner)))
    return pairs


def sends_last(axis):
    even = lax.axis_index(axis) % 2 == 0
    return even if lax.axis_size(axis) <= 2 else (lax.axis_index("chan") == 0) == even


def traded(value, axis):
    size = lax.axis_size(axis)
    if size == 1:
        return jnp.zeros_like(value), jnp.zeros_like(value)
    if size == 2:
        got = lax.ppermute(value, axis, swaps(size, 1))
        return got, got
    pairs = shared_pairs(axis, lax.axis_size("tiles"), lax.axis_size("rows"))
    got = lax.ppermute(value, ("tiles", "rows", "chan"), pairs)
    return got, core_swapped(got)


def before_and_after(got, other, axis):
    index, none = lax.axis_index(axis), jnp.zeros_like(got)
    last = sends_last(axis)
    before = jnp.where(index == 0, none, jnp.where(last, other, got))
    after = jnp.where(index == lax.axis_size(axis) - 1, none, jnp.where(last, got, other))
    return before, after


def roll_columns(value, amount):
    return pltpu.roll(value, amount % SLOTS, axis=1)


def prepare_kernel(
    n_rows,
    count_ref,
    order_hbm,
    cot_hbm,
    w1_hbm,
    w2_hbm,
    shift_hbm,
    near_ref,
    edge_ref,
    w2_ref,
    wa_ref,
    shift_ref,
    cot,
    w1,
    order,
    rank,
    sems,
):
    rows, cols, half = cot.shape
    pairs = [
        (order_hbm, order),
        (cot_hbm, cot),
        (w1_hbm, w1),
        (w2_hbm, w2_ref),
        (shift_hbm, shift_ref),
    ]
    copies = [pltpu.make_async_copy(a, b, sems.at[i]) for i, (a, b) in enumerate(pairs)]
    for copy in copies:
        copy.start()
    copies[0].wait()
    for k in range(order.shape[2]):
        rank[order[0, 0, k]] = k
    side = TP // 2
    across = cols // side
    col_id = lax.broadcasted_iota(jnp.int32, (cols, 2 * half), 0)
    lane_id = lax.broadcasted_iota(jnp.int32, (cols, 2 * half), 1)
    mine = (lane_id < half) == (lax.axis_index("chan") == 0)
    masks = []
    for a in range(rows // side):
        place = jnp.zeros((cols, 2 * half), jnp.int32)
        for b in range(across):
            inside = (col_id >= b * side) & (col_id < (b + 1) * side)
            place = jnp.where(inside, rank[a * across + b], place)
        masks.append((place < count_ref[0:1, :]) & mine)
    copies[1].wait()
    lower = lax.axis_index("rows") % 2 == 0
    kept = []
    for i in range(rows):
        value = cot[i].astype(F32)
        twice = jnp.concatenate([value, value], axis=1)
        placed = jnp.where(masks[i // side], twice, 0.0)
        near_ref[i] = placed.astype(BF)
        kept.append(placed)
    for i in range(3):
        top, bottom = kept[i], kept[rows - 3 + i]
        at = slice(i * cols, (i + 1) * cols)
        if n_rows == 2:
            edge_ref[0, at, :] = jnp.where(lower, bottom, top).astype(BF)
        else:
            edge_ref[0, at, :] = top.astype(BF)
            edge_ref[1, at, :] = bottom.astype(BF)
    copies[2].wait()
    lanes = 2 * half
    for u in range(3):
        low = slice(u * lanes, u * lanes + half)
        high = slice(u * lanes + half, (u + 1) * lanes)
        wa_ref[low, :lanes] = jnp.zeros((half, lanes), BF)
        wa_ref[high, :lanes] = w1[u, 0]
        wa_ref[low, lanes:] = w1[u, 1]
        wa_ref[high, lanes:] = w1[u, 2]
    copies[3].wait()
    copies[4].wait()


def flat(value):
    return value.reshape(value.shape[0] * SLOTS, value.shape[2])


def image(value):
    return value.reshape(value.shape[0] // SLOTS, SLOTS, value.shape[1])


def block_place():
    return lax.axis_index("tiles") % 2 * 2 + lax.axis_index("rows") % 2


def main_kernel(
    n_tiles,
    n_rows,
    picture_ref,
    near_ref,
    far_ref,
    own_w2_ref,
    other_w2_ref,
    before_ref,
    after_ref,
    got_ref,
    got_other_ref,
    wa_ref,
    shift_ref,
    mid_ref,
    weight_ref,
    a_ref,
    u_ref,
    w2_ref,
):
    rows = u_ref.shape[0] - 6
    height, own_cols, lanes = picture_ref.shape
    tall = rows + 1
    half = lanes // 2
    row_index, tile_index = lax.axis_index("rows"), lax.axis_index("tiles")
    low = lax.axis_index("chan") == 0

    a_ref[0, :, :own_cols] = before_ref[:2]
    a_ref[rows + 1, :, :own_cols] = after_ref[:2]
    u_ref[:3, :own_cols] = before_ref[2:]
    u_ref[rows + 3 :, :own_cols] = after_ref[2:]
    for i in range(rows):
        a_ref[i + 1, :, :own_cols] = picture_ref[2 * i : 2 * i + 2]
        u_ref[i + 3, :own_cols] = near_ref[i] + far_ref[i]
    got, shared = got_ref[...].astype(F32), got_other_ref[...].astype(F32)
    mine_after = tile_index % 2 == 0
    if n_tiles > 2:
        mine_after = low == mine_after
        left_strip, right_strip = jnp.where(mine_after, shared, got), jnp.where(mine_after, got, shared)
    else:
        left_strip = right_strip = got
    left_strip = jnp.where(tile_index == 0, 0.0, left_strip)
    right_strip = jnp.where(tile_index == n_tiles - 1, 0.0, right_strip)

    def edge(at, count):
        fill = jnp.zeros((SLOTS - own_cols - 2 * count, lanes), F32)
        value = [right_strip[at : at + count], fill, left_strip[at : at + count]]
        return jnp.concatenate(value, axis=0).astype(BF)

    own_u, halo_a, halo_u = height, height + 4 * rows, height + 4 * rows + 4
    for i in range(height):
        a_ref[i // 2 + 1, i % 2, own_cols:] = edge(i, 1)
    for i in range(2):
        a_ref[0, i, own_cols:] = edge(halo_a + i, 1)
        a_ref[rows + 1, i, own_cols:] = edge(halo_a + 2 + i, 1)
    for i in range(rows):
        u_ref[i + 3, own_cols:] = edge(own_u + 4 * i, 4)
    for i in range(3):
        u_ref[i, own_cols:] = edge(halo_u + 4 * i, 4)
        u_ref[rows + 3 + i, own_cols:] = edge(halo_u + 12 + 4 * i, 4)

    def a_rows(count):
        return jnp.concatenate(
            [
                flat(a_ref[0:count, 1]),
                flat(a_ref[1 : count + 1, 0]),
                flat(a_ref[1 : count + 1, 1]),
            ],
            axis=1,
        )

    def u_rows(count):
        return jnp.concatenate([flat(u_ref[5 - 2 * u : 5 - 2 * u + count]) for u in range(3)], axis=1)

    for u in range(3):
        for w in range(3):
            at = slice((u * 3 + w) * half, (u * 3 + w + 1) * half)
            own_w, other_w = own_w2_ref[at, :], other_w2_ref[at, :]
            across = slice(w * lanes, (w + 1) * lanes)
            w2_ref[u * lanes : u * lanes + half, across] = jnp.where(low, own_w, other_w)
            w2_ref[u * lanes + half : (u + 1) * lanes, across] = jnp.where(low, other_w, own_w)

    row_id = lax.broadcasted_iota(jnp.int32, (tall, SLOTS, lanes), 0)
    col_id = lax.broadcasted_iota(jnp.int32, (tall, SLOTS, lanes), 1)
    own = (row_id < rows) & (col_id < own_cols)
    last_row = rows + jnp.where(row_index < n_rows - 1, 1, 0)
    last_col = own_cols + jnp.where(tile_index < n_tiles - 1, 1, 0)
    valid = (row_id < last_row) & (col_id < last_col)

    wa = wa_ref[...]
    part = jnp.dot(a_rows(tall), wa, preferred_element_type=F32)
    pre = image(part[:, lanes:]) + roll_columns(image(part[:, :lanes]), 1) + shift_ref[0]
    middle = jnp.maximum(pre, 0.0).astype(BF).astype(F32)

    mid_part = jnp.dot(u_rows(tall), w2_ref[...], preferred_element_type=F32)
    mid_raw = (
        roll_columns(image(mid_part[:, :lanes]), -2)
        + image(mid_part[:, lanes : 2 * lanes])
        + roll_columns(image(mid_part[:, 2 * lanes :]), 2)
    )
    mid_grad = jnp.where((middle > 0) & valid, mid_raw, 0.0)
    mid_ref[...] = mid_grad.astype(BF)

    middle_own = jnp.where(own, middle, 0.0)[:rows]
    middle_taps = jnp.concatenate(
        [
            flat(roll_columns(middle_own, 2)).astype(BF),
            flat(middle_own).astype(BF),
            flat(roll_columns(middle_own, -2)).astype(BF),
        ],
        axis=1,
    )
    over_pixels = (((0,), (0,)), ((), ()))
    second = lax.dot_general(u_rows(rows), middle_taps, over_pixels, preferred_element_type=F32)

    grad_own = jnp.where(own, mid_grad, 0.0)[:rows]
    grad_taps = jnp.concatenate(
        [flat(roll_columns(grad_own, -1)).astype(BF), flat(grad_own).astype(BF)], axis=1
    )
    first = lax.dot_general(a_rows(rows), grad_taps, over_pixels, preferred_element_type=F32)

    left = lax.broadcasted_iota(jnp.int32, (half, lanes), 1) < half

    part = weight_ref.shape[1]
    me = block_place()

    def keep(block, value):
        done = 0
        while done < half:
            number, at = divmod(block * half + done, part)
            count = min(part - at, half - done)
            weight_ref[number ^ me, at : at + count, :] = value[done : done + count].astype(BF)
            done += count

    def at_left(value):
        return jnp.where(low, value, pltpu.roll(value, half, axis=1))

    def at_right(value):
        return jnp.where(low, pltpu.roll(value, half, axis=1), value)

    centre = []
    for u in range(3):
        top = u * lanes
        for w in range(3):
            across = slice(w * lanes, (w + 1) * lanes)
            keep(
                u * 3 + w,
                jnp.where(low, second[top : top + half, across], second[top + half : top + lanes, across]),
            )
        outer = first[top + half : top + lanes]
        keep(9 + u, jnp.where(left, at_left(outer[:, :lanes]), at_right(outer[:, lanes:])))
        centre.append(first[top : top + half, lanes:])
    keep(12, jnp.where(left, at_left(centre[0]), at_right(centre[1])))
    keep(13, at_left(centre[2]))


def input_kernel(mid_ref, wa_ref, grad_ref):
    rows, own_cols, lanes = grad_ref.shape[0], grad_ref.shape[2], grad_ref.shape[3]
    tall = rows + 1
    by_lanes = (((1,), (1,)), ((), ()))
    grads = flat(mid_ref[...])
    wa = wa_ref[...]
    straight = lax.dot_general(grads, wa[:, lanes:], by_lanes, preferred_element_type=F32)
    shifted = lax.dot_general(grads, wa[:, :lanes], by_lanes, preferred_element_type=F32)

    def taps(u):
        s = slice(u * lanes, (u + 1) * lanes)
        return image(straight[:, s]) + roll_columns(image(shifted[:, s]), -1)

    above, level, below = taps(0), taps(1), taps(2)
    grad_ref[:, 0] = level[:rows, :own_cols].astype(BF)
    grad_ref[:, 1] = (below[:rows, :own_cols] + above[1:tall, :own_cols]).astype(BF)


def unpack_kernel(scale, piece_0, piece_1, piece_2, piece_3, first_ref, second_ref, all_ref):
    half = first_ref.shape[2]
    part = piece_0.shape[0]
    me = block_place()
    for distance, piece in enumerate((piece_0, piece_1, piece_2, piece_3)):
        all_ref[me ^ distance] = piece[...]

    def block(number):
        done, values = 0, []
        while done < half:
            which, at = divmod(number * half + done, part)
            count = min(part - at, half - done)
            values.append(all_ref[which, at : at + count, :].astype(F32) * scale)
            done += count
        return values[0] if len(values) == 1 else jnp.concatenate(values, axis=0)

    for tap in range(9):
        second_ref[tap] = block(tap)
    for u in range(3):
        value = block(9 + u)
        first_ref[3 * u] = value[:, :half]
        first_ref[3 * u + 2] = value[:, half:]
    value = block(12)
    first_ref[1] = value[:, :half]
    first_ref[4] = value[:, half:]
    first_ref[7] = block(13)[:, :half]


def summed_pair(value, axis, size, distance):
    got = lax.ppermute(value, axis, swaps(size, distance))
    return (value.astype(F32) + got.astype(F32)).astype(BF)


def shards(acts, shift, weight_one, weight_two, cotangent, tissue_count, tile_order):
    channels, mids = weight_one.shape[2], weight_one.shape[3]
    height = acts.shape[0]
    lanes = 2 * channels
    pairs = acts.shape[1] // lanes
    rows, cols = height // 2, pairs
    tile_rows, tile_cols = height // TP, 2 * pairs // TP
    out_side = TP // 2
    n_rows, n_tiles = lax.axis_size("rows"), lax.axis_size("tiles")

    whole = pl.BlockSpec(memory_space=pltpu.VMEM)
    in_hbm = pl.BlockSpec(memory_space=pltpu.HBM)
    limit = pltpu.CompilerParams(vmem_limit_bytes=48 << 20)
    half = channels
    n_edges = 1 if n_rows == 2 else 2
    near, edges, own_w2, wa, shift_row = pl.pallas_call(
        functools.partial(prepare_kernel, n_rows),
        out_shape=(
            jax.ShapeDtypeStruct((rows, cols, lanes), BF),
            jax.ShapeDtypeStruct((n_edges, 3 * cols, lanes), BF),
            jax.ShapeDtypeStruct((9 * half, mids), BF),
            jax.ShapeDtypeStruct((3 * lanes, 2 * mids), BF),
            jax.ShapeDtypeStruct((1, mids), F32),
        ),
        in_specs=[whole] + [in_hbm] * 5,
        out_specs=(whole,) * 5,
        scratch_shapes=[
            pltpu.VMEM((rows, cols, half), BF),
            pltpu.VMEM((3, 3, channels, mids), BF),
            pltpu.SMEM((1, 1, tile_rows * tile_cols), jnp.int32),
            pltpu.SMEM((tile_rows * tile_cols,), jnp.int32),
            pltpu.SemaphoreType.DMA((5,)),
        ],
        compiler_params=limit,
    )(
        jnp.broadcast_to(tissue_count, (8, lanes)),
        *(
            pltpu.with_memory_space_constraint(value, pltpu.HBM)
            for value in (
                tile_order,
                cotangent,
                weight_one,
                weight_two.swapaxes(2, 3).reshape(9 * half, mids),
                shift.reshape(1, mids),
            )
        ),
    )
    if n_rows == 2:
        edge_u = edges[0] + core_swapped(edges[0])
    else:
        edges = edges + core_swapped(edges)
        edge_u = jnp.where(sends_last("rows"), edges[1], edges[0])
    picture = acts.reshape(height, pairs, lanes)
    edge_a = jnp.where(sends_last("rows"), picture[height - 2 :], picture[:2])
    before, after = (
        value.reshape(5, cols, lanes)
        for value in before_and_after(
            *traded(jnp.concatenate([edge_a.reshape(2 * cols, lanes), edge_u], axis=0), "rows"),
            "rows",
        )
    )
    far = core_swapped(near)
    own_w2, before = lax.optimization_barrier((own_w2, before))
    other_w2 = core_swapped(own_w2)

    right = sends_last("tiles")
    side = lambda value, count: jnp.where(
        right, value[:, cols - count :], value[:, :count]
    ).reshape(count * value.shape[0], lanes)
    got, got_other = traded(
        jnp.concatenate(
            [
                side(picture, 1),
                side(near, 4) + side(far, 4),
                side(before[:2], 1),
                side(after[:2], 1),
                side(before[2:], 4),
                side(after[2:], 4),
            ],
            axis=0,
        ),
        "tiles",
    )

    part = 14 * half // 4
    mid_grad, weights = pl.pallas_call(
        functools.partial(main_kernel, n_tiles, n_rows),
        out_shape=(
            jax.ShapeDtypeStruct((rows + 1, SLOTS, lanes), BF),
            jax.ShapeDtypeStruct((4, part, lanes), BF),
        ),
        in_specs=[whole] * 11,
        out_specs=(whole, whole),
        scratch_shapes=[
            pltpu.VMEM((rows + 2, 2, SLOTS, lanes), BF),
            pltpu.VMEM((rows + 6, SLOTS, lanes), BF),
            pltpu.VMEM((3 * lanes, 3 * mids), BF),
        ],
        compiler_params=limit,
    )(picture, near, far, own_w2, other_w2, before, after, got, got_other, wa, shift_row)
    input_grad = pl.pallas_call(
        input_kernel,
        out_shape=jax.ShapeDtypeStruct((rows, 2, cols, lanes), BF),
        in_specs=[whole, whole],
        out_specs=whole,
        compiler_params=limit,
    )(mid_grad, wa)

    def from_block(values):
        return [
            lax.ppermute(
                value,
                ("tiles", "rows"),
                [
                    (t * n_rows + r, (t ^ (d >> 1)) * n_rows + (r ^ (d & 1)))
                    for t in range(n_tiles)
                    for r in range(n_rows)
                ],
            )
            for d, value in enumerate(values, 1)
        ]

    one, two, three = from_block([weights[1], weights[2], weights[3]])
    total = (
        (weights[0].astype(F32) + one.astype(F32)) + (two.astype(F32) + three.astype(F32))
    ).astype(BF)
    distance = 2
    while distance < n_rows:
        total = summed_pair(total, "rows", n_rows, distance)
        distance *= 2
    distance = 2
    while distance < n_tiles:
        total = summed_pair(total, "tiles", n_tiles, distance)
        distance *= 2
    pieces = [total] + from_block([total] * 3)

    pixels = n_rows * TISS_MEAN * n_tiles * out_side * out_side
    scale = 1.0 / math.sqrt(pixels)
    first, second = pl.pallas_call(
        functools.partial(unpack_kernel, scale),
        out_shape=(
            jax.ShapeDtypeStruct((9, channels, half), F32),
            jax.ShapeDtypeStruct((9, half, mids), F32),
        ),
        in_specs=[whole] * 4,
        out_specs=(whole, whole),
        scratch_shapes=[pltpu.VMEM((4, part, lanes), BF)],
        compiler_params=limit,
    )(*pieces)
    return (
        input_grad.reshape(height, pairs * lanes),
        first.reshape(3, 3, channels, half),
        second.reshape(3, 3, half, mids).swapaxes(2, 3),
    )


def solution(mesh):
    return jax.shard_map(
        shards,
        mesh=mesh,
        in_specs=(
            P(("groups", "rows"), "tiles"),
            P(),
            P(),
            P(None, None, None, "chan"),
            P(("groups", "rows"), "tiles", "chan"),
            P(("groups", "rows"), "tiles"),
            P(("groups", "rows"), "tiles", None),
        ),
        out_specs=(
            P(("groups", "rows"), "tiles"),
            P("groups", None, None, "chan"),
            P("groups", None, None, "chan"),
        ),
        check_vma=False,
    )
```

```python
import functools
import math

import jax
import jax.numpy as jnp
from jax import lax
from jax.experimental import pallas as pl
from jax.experimental.pallas import tpu as pltpu
from jax.sharding import PartitionSpec as P

TP = 12
TISS_MEAN = 8
BF = jnp.bfloat16
F32 = jnp.float32
SLOTS = 64


def swaps(size, distance):
    return [(i, i ^ distance) for i in range(size) if (i ^ distance) < size]


def core_swapped(value):
    return lax.ppermute(value, "chan", [(0, 1), (1, 0)])


def shared_pairs(axis, n_tiles, n_rows):
    sizes = (n_tiles, n_rows)
    along = ("tiles", "rows").index(axis)
    size = sizes[along]
    pairs = []
    for t in range(n_tiles):
        for r in range(n_rows):
            for core in range(2):
                place, partner = [t, r], [t, r]
                if core == 0:
                    partner[along] = place[along] ^ 1
                else:
                    partner[along] = ((place[along] + 1) ^ 1) - 1
                if not 0 <= partner[along] < size:
                    partner[along] = place[along]
                    partner[1 - along] = place[1 - along] ^ 1
                    if partner[1 - along] >= sizes[1 - along]:
                        continue
                code = lambda p: (p[0] * n_rows + p[1]) * 2 + core
                pairs.append((code(place), code(partner)))
    return pairs


def sends_last(axis):
    even = lax.axis_index(axis) % 2 == 0
    return even if lax.axis_size(axis) <= 2 else (lax.axis_index("chan") == 0) == even


def traded(value, axis):
    size = lax.axis_size(axis)
    if size == 1:
        return jnp.zeros_like(value), jnp.zeros_like(value)
    if size == 2:
        got = lax.ppermute(value, axis, swaps(size, 1))
        return got, got
    pairs = shared_pairs(axis, lax.axis_size("tiles"), lax.axis_size("rows"))
    got = lax.ppermute(value, ("tiles", "rows", "chan"), pairs)
    return got, core_swapped(got)


def before_and_after(got, other, axis):
    index, none = lax.axis_index(axis), jnp.zeros_like(got)
    last = sends_last(axis)
    before = jnp.where(index == 0, none, jnp.where(last, other, got))
    after = jnp.where(index == lax.axis_size(axis) - 1, none, jnp.where(last, got, other))
    return before, after


def roll_columns(value, amount):
    return pltpu.roll(value, amount % SLOTS, axis=1)


def prepare_kernel(
    n_rows,
    order_hbm,
    cot_hbm,
    w1_hbm,
    w2_hbm,
    shift_hbm,
    near_ref,
    edge_ref,
    place_ref,
    w2_ref,
    wa_ref,
    shift_ref,
    cot,
    w1,
    order,
    rank,
    sems,
):
    rows, cols, half = cot.shape
    pairs = [
        (order_hbm, order),
        (cot_hbm, cot),
        (w1_hbm, w1),
        (w2_hbm, w2_ref),
        (shift_hbm, shift_ref),
    ]
    copies = [pltpu.make_async_copy(a, b, sems.at[i]) for i, (a, b) in enumerate(pairs)]
    for copy in copies:
        copy.start()
    copies[0].wait()
    for k in range(order.shape[2]):
        rank[order[0, 0, k]] = k
    side = TP // 2
    across = cols // side
    col_id = lax.broadcasted_iota(jnp.int32, (cols, 2 * half), 0)
    lane_id = lax.broadcasted_iota(jnp.int32, (cols, 2 * half), 1)
    mine = (lane_id < half) == (lax.axis_index("chan") == 0)
    for a in range(rows // side):
        place = jnp.zeros((cols, 2 * half), jnp.int32)
        for b in range(across):
            inside = (col_id >= b * side) & (col_id < (b + 1) * side)
            place = jnp.where(inside, rank[a * across + b], place)
        place_ref[a] = place
    copies[1].wait()
    lower = lax.axis_index("rows") % 2 == 0
    kept = []
    for i in range(rows):
        value = cot[i].astype(F32)
        placed = jnp.where(mine, jnp.concatenate([value, value], axis=1), 0.0)
        near_ref[i] = placed.astype(BF)
        kept.append(placed)
    for i in range(3):
        top, bottom = kept[i], kept[rows - 3 + i]
        at = slice(i * cols, (i + 1) * cols)
        if n_rows == 2:
            edge_ref[0, at, :] = jnp.where(lower, bottom, top).astype(BF)
        else:
            edge_ref[0, at, :] = top.astype(BF)
            edge_ref[1, at, :] = bottom.astype(BF)
    copies[2].wait()
    lanes = 2 * half
    for u in range(3):
        low = slice(u * lanes, u * lanes + half)
        high = slice(u * lanes + half, (u + 1) * lanes)
        wa_ref[low, :lanes] = jnp.zeros((half, lanes), BF)
        wa_ref[high, :lanes] = w1[u, 0]
        wa_ref[low, lanes:] = w1[u, 1]
        wa_ref[high, lanes:] = w1[u, 2]
    copies[3].wait()
    copies[4].wait()


def flat(value):
    return value.reshape(value.shape[0] * SLOTS, value.shape[2])


def image(value):
    return value.reshape(value.shape[0] // SLOTS, SLOTS, value.shape[1])


def block_place():
    return lax.axis_index("tiles") % 2 * 2 + lax.axis_index("rows") % 2


def main_kernel(
    n_tiles,
    n_rows,
    picture_ref,
    near_ref,
    far_ref,
    own_w2_ref,
    other_w2_ref,
    before_ref,
    after_ref,
    got_ref,
    got_other_ref,
    wa_ref,
    shift_ref,
    mid_ref,
    weight_ref,
    a_ref,
    u_ref,
    w2_ref,
):
    rows = u_ref.shape[0] - 6
    height, own_cols, lanes = picture_ref.shape
    tall = rows + 1
    half = lanes // 2
    row_index, tile_index = lax.axis_index("rows"), lax.axis_index("tiles")
    low = lax.axis_index("chan") == 0

    a_ref[0, :, :own_cols] = before_ref[:2]
    a_ref[rows + 1, :, :own_cols] = after_ref[:2]
    u_ref[:3, :own_cols] = before_ref[2:]
    u_ref[rows + 3 :, :own_cols] = after_ref[2:]
    for i in range(rows):
        a_ref[i + 1, :, :own_cols] = picture_ref[2 * i : 2 * i + 2]
        u_ref[i + 3, :own_cols] = near_ref[i] + far_ref[i]
    got, shared = got_ref[...].astype(F32), got_other_ref[...].astype(F32)
    mine_after = tile_index % 2 == 0
    if n_tiles > 2:
        mine_after = low == mine_after
        left_strip, right_strip = jnp.where(mine_after, shared, got), jnp.where(mine_after, got, shared)
    else:
        left_strip = right_strip = got
    left_strip = jnp.where(tile_index == 0, 0.0, left_strip)
    right_strip = jnp.where(tile_index == n_tiles - 1, 0.0, right_strip)

    def edge(at, count):
        fill = jnp.zeros((SLOTS - own_cols - 2 * count, lanes), F32)
        value = [right_strip[at : at + count], fill, left_strip[at : at + count]]
        return jnp.concatenate(value, axis=0).astype(BF)

    own_u, halo_a, halo_u = height, height + 4 * rows, height + 4 * rows + 4
    for i in range(height):
        a_ref[i // 2 + 1, i % 2, own_cols:] = edge(i, 1)
    for i in range(2):
        a_ref[0, i, own_cols:] = edge(halo_a + i, 1)
        a_ref[rows + 1, i, own_cols:] = edge(halo_a + 2 + i, 1)
    for i in range(rows):
        u_ref[i + 3, own_cols:] = edge(own_u + 4 * i, 4)
    for i in range(3):
        u_ref[i, own_cols:] = edge(halo_u + 4 * i, 4)
        u_ref[rows + 3 + i, own_cols:] = edge(halo_u + 12 + 4 * i, 4)

    def a_rows(count):
        return jnp.concatenate(
            [
                flat(a_ref[0:count, 1]),
                flat(a_ref[1 : count + 1, 0]),
                flat(a_ref[1 : count + 1, 1]),
            ],
            axis=1,
        )

    def u_rows(count):
        return jnp.concatenate([flat(u_ref[5 - 2 * u : 5 - 2 * u + count]) for u in range(3)], axis=1)

    for u in range(3):
        for w in range(3):
            at = slice((u * 3 + w) * half, (u * 3 + w + 1) * half)
            own_w, other_w = own_w2_ref[at, :], other_w2_ref[at, :]
            across = slice(w * lanes, (w + 1) * lanes)
            w2_ref[u * lanes : u * lanes + half, across] = jnp.where(low, own_w, other_w)
            w2_ref[u * lanes + half : (u + 1) * lanes, across] = jnp.where(low, other_w, own_w)

    row_id = lax.broadcasted_iota(jnp.int32, (tall, SLOTS, lanes), 0)
    col_id = lax.broadcasted_iota(jnp.int32, (tall, SLOTS, lanes), 1)
    own = (row_id < rows) & (col_id < own_cols)
    last_row = rows + jnp.where(row_index < n_rows - 1, 1, 0)
    last_col = own_cols + jnp.where(tile_index < n_tiles - 1, 1, 0)
    valid = (row_id < last_row) & (col_id < last_col)

    wa = wa_ref[...]
    part = jnp.dot(a_rows(tall), wa, preferred_element_type=F32)
    pre = image(part[:, lanes:]) + roll_columns(image(part[:, :lanes]), 1) + shift_ref[0]
    middle = jnp.maximum(pre, 0.0).astype(BF).astype(F32)

    mid_part = jnp.dot(u_rows(tall), w2_ref[...], preferred_element_type=F32)
    mid_raw = (
        roll_columns(image(mid_part[:, :lanes]), -2)
        + image(mid_part[:, lanes : 2 * lanes])
        + roll_columns(image(mid_part[:, 2 * lanes :]), 2)
    )
    mid_grad = jnp.where((middle > 0) & valid, mid_raw, 0.0)
    mid_ref[...] = mid_grad.astype(BF)

    middle_own = jnp.where(own, middle, 0.0)[:rows]
    middle_taps = jnp.concatenate(
        [
            flat(roll_columns(middle_own, 2)).astype(BF),
            flat(middle_own).astype(BF),
            flat(roll_columns(middle_own, -2)).astype(BF),
        ],
        axis=1,
    )
    over_pixels = (((0,), (0,)), ((), ()))
    second = lax.dot_general(u_rows(rows), middle_taps, over_pixels, preferred_element_type=F32)

    grad_own = jnp.where(own, mid_grad, 0.0)[:rows]
    grad_taps = jnp.concatenate(
        [flat(roll_columns(grad_own, -1)).astype(BF), flat(grad_own).astype(BF)], axis=1
    )
    first = lax.dot_general(a_rows(rows), grad_taps, over_pixels, preferred_element_type=F32)

    left = lax.broadcasted_iota(jnp.int32, (half, lanes), 1) < half

    part = weight_ref.shape[1]
    me = block_place()

    def keep(block, value):
        done = 0
        while done < half:
            number, at = divmod(block * half + done, part)
            count = min(part - at, half - done)
            weight_ref[number ^ me, at : at + count, :] = value[done : done + count].astype(BF)
            done += count

    def at_left(value):
        return jnp.where(low, value, pltpu.roll(value, half, axis=1))

    def at_right(value):
        return jnp.where(low, pltpu.roll(value, half, axis=1), value)

    centre = []
    for u in range(3):
        top = u * lanes
        for w in range(3):
            across = slice(w * lanes, (w + 1) * lanes)
            keep(
                u * 3 + w,
                jnp.where(low, second[top : top + half, across], second[top + half : top + lanes, across]),
            )
        outer = first[top + half : top + lanes]
        keep(9 + u, jnp.where(left, at_left(outer[:, :lanes]), at_right(outer[:, lanes:])))
        centre.append(first[top : top + half, lanes:])
    keep(12, jnp.where(left, at_left(centre[0]), at_right(centre[1])))
    keep(13, at_left(centre[2]))


def input_kernel(mid_ref, wa_ref, grad_ref):
    rows, own_cols, lanes = grad_ref.shape[0], grad_ref.shape[2], grad_ref.shape[3]
    tall = rows + 1
    by_lanes = (((1,), (1,)), ((), ()))
    grads = flat(mid_ref[...])
    wa = wa_ref[...]
    straight = lax.dot_general(grads, wa[:, lanes:], by_lanes, preferred_element_type=F32)
    shifted = lax.dot_general(grads, wa[:, :lanes], by_lanes, preferred_element_type=F32)

    def taps(u):
        s = slice(u * lanes, (u + 1) * lanes)
        return image(straight[:, s]) + roll_columns(image(shifted[:, s]), -1)

    above, level, below = taps(0), taps(1), taps(2)
    grad_ref[:, 0] = level[:rows, :own_cols].astype(BF)
    grad_ref[:, 1] = (below[:rows, :own_cols] + above[1:tall, :own_cols]).astype(BF)


def unpack_kernel(scale, piece_0, piece_1, piece_2, piece_3, first_ref, second_ref, all_ref):
    half = first_ref.shape[2]
    part = piece_0.shape[0]
    me = block_place()
    for distance, piece in enumerate((piece_0, piece_1, piece_2, piece_3)):
        all_ref[me ^ distance] = piece[...]

    def block(number):
        done, values = 0, []
        while done < half:
            which, at = divmod(number * half + done, part)
            count = min(part - at, half - done)
            values.append(all_ref[which, at : at + count, :].astype(F32) * scale)
            done += count
        return values[0] if len(values) == 1 else jnp.concatenate(values, axis=0)

    for tap in range(9):
        second_ref[tap] = block(tap)
    for u in range(3):
        value = block(9 + u)
        first_ref[3 * u] = value[:, :half]
        first_ref[3 * u + 2] = value[:, half:]
    value = block(12)
    first_ref[1] = value[:, :half]
    first_ref[4] = value[:, half:]
    first_ref[7] = block(13)[:, :half]


def summed_pair(value, axis, size, distance):
    got = lax.ppermute(value, axis, swaps(size, distance))
    return (value.astype(F32) + got.astype(F32)).astype(BF)


def shards(acts, shift, weight_one, weight_two, cotangent, tissue_count, tile_order):
    channels, mids = weight_one.shape[2], weight_one.shape[3]
    height = acts.shape[0]
    lanes = 2 * channels
    pairs = acts.shape[1] // lanes
    rows, cols = height // 2, pairs
    tile_rows, tile_cols = height // TP, 2 * pairs // TP
    out_side = TP // 2
    n_rows, n_tiles = lax.axis_size("rows"), lax.axis_size("tiles")

    whole = pl.BlockSpec(memory_space=pltpu.VMEM)
    in_hbm = pl.BlockSpec(memory_space=pltpu.HBM)
    limit = pltpu.CompilerParams(vmem_limit_bytes=48 << 20)
    half = channels
    n_edges = 1 if n_rows == 2 else 2
    near, edges, place, own_w2, wa, shift_row = pl.pallas_call(
        functools.partial(prepare_kernel, n_rows),
        out_shape=(
            jax.ShapeDtypeStruct((rows, cols, lanes), BF),
            jax.ShapeDtypeStruct((n_edges, 3 * cols, lanes), BF),
            jax.ShapeDtypeStruct((tile_rows, cols, lanes), jnp.int32),
            jax.ShapeDtypeStruct((9 * half, mids), BF),
            jax.ShapeDtypeStruct((3 * lanes, 2 * mids), BF),
            jax.ShapeDtypeStruct((1, mids), F32),
        ),
        in_specs=[in_hbm] * 5,
        out_specs=(whole,) * 6,
        scratch_shapes=[
            pltpu.VMEM((rows, cols, half), BF),
            pltpu.VMEM((3, 3, channels, mids), BF),
            pltpu.SMEM((1, 1, tile_rows * tile_cols), jnp.int32),
            pltpu.SMEM((tile_rows * tile_cols,), jnp.int32),
            pltpu.SemaphoreType.DMA((5,)),
        ],
        compiler_params=limit,
    )(
        *(
            pltpu.with_memory_space_constraint(value, pltpu.HBM)
            for value in (
                tile_order,
                cotangent,
                weight_one,
                weight_two.swapaxes(2, 3).reshape(9 * half, mids),
                shift.reshape(1, mids),
            )
        ),
    )
    other_edges = core_swapped(edges)
    edges, tissue_count = lax.optimization_barrier((edges, tissue_count))
    live = place < tissue_count[0, 0]
    near = jnp.where(live[:, None], near.reshape(tile_rows, -1, cols, lanes), jnp.zeros((), BF))
    near = near.reshape(rows, cols, lanes)
    edges = (edges + other_edges).reshape(n_edges, 3, cols, lanes)
    last = sends_last("rows")
    edge_u = edges[0] if n_rows == 2 else jnp.where(last, edges[1], edges[0])
    edge_u = jnp.where(jnp.where(last, live[-1], live[0]), edge_u, jnp.zeros((), BF))
    edge_u = edge_u.reshape(3 * cols, lanes)
    picture = acts.reshape(height, pairs, lanes)
    edge_a = jnp.where(last, picture[height - 2 :], picture[:2])
    strip = jnp.concatenate([edge_a.reshape(2 * cols, lanes), edge_u], axis=0)
    strip, near = lax.optimization_barrier((strip, near))
    before, after = (
        value.reshape(5, cols, lanes)
        for value in before_and_after(*traded(strip, "rows"), "rows")
    )
    far = core_swapped(near)
    own_w2, before = lax.optimization_barrier((own_w2, before))
    other_w2 = core_swapped(own_w2)

    right = sends_last("tiles")
    side = lambda value, count: jnp.where(
        right, value[:, cols - count :], value[:, :count]
    ).reshape(count * value.shape[0], lanes)
    got, got_other = traded(
        jnp.concatenate(
            [
                side(picture, 1),
                side(near, 4) + side(far, 4),
                side(before[:2], 1),
                side(after[:2], 1),
                side(before[2:], 4),
                side(after[2:], 4),
            ],
            axis=0,
        ),
        "tiles",
    )

    part = 14 * half // 4
    mid_grad, weights = pl.pallas_call(
        functools.partial(main_kernel, n_tiles, n_rows),
        out_shape=(
            jax.ShapeDtypeStruct((rows + 1, SLOTS, lanes), BF),
            jax.ShapeDtypeStruct((4, part, lanes), BF),
        ),
        in_specs=[whole] * 11,
        out_specs=(whole, whole),
        scratch_shapes=[
            pltpu.VMEM((rows + 2, 2, SLOTS, lanes), BF),
            pltpu.VMEM((rows + 6, SLOTS, lanes), BF),
            pltpu.VMEM((3 * lanes, 3 * mids), BF),
        ],
        compiler_params=limit,
    )(picture, near, far, own_w2, other_w2, before, after, got, got_other, wa, shift_row)
    input_grad = pl.pallas_call(
        input_kernel,
        out_shape=jax.ShapeDtypeStruct((rows, 2, cols, lanes), BF),
        in_specs=[whole, whole],
        out_specs=whole,
        compiler_params=limit,
    )(mid_grad, wa)

    def from_block(values):
        return [
            lax.ppermute(
                value,
                ("tiles", "rows"),
                [
                    (t * n_rows + r, (t ^ (d >> 1)) * n_rows + (r ^ (d & 1)))
                    for t in range(n_tiles)
                    for r in range(n_rows)
                ],
            )
            for d, value in enumerate(values, 1)
        ]

    one, two, three = from_block([weights[1], weights[2], weights[3]])
    total = (
        (weights[0].astype(F32) + one.astype(F32)) + (two.astype(F32) + three.astype(F32))
    ).astype(BF)
    distance = 2
    while distance < n_rows:
        total = summed_pair(total, "rows", n_rows, distance)
        distance *= 2
    distance = 2
    while distance < n_tiles:
        total = summed_pair(total, "tiles", n_tiles, distance)
        distance *= 2
    pieces = [total] + from_block([total] * 3)

    pixels = n_rows * TISS_MEAN * n_tiles * out_side * out_side
    scale = 1.0 / math.sqrt(pixels)
    first, second = pl.pallas_call(
        functools.partial(unpack_kernel, scale),
        out_shape=(
            jax.ShapeDtypeStruct((9, channels, half), F32),
            jax.ShapeDtypeStruct((9, half, mids), F32),
        ),
        in_specs=[whole] * 4,
        out_specs=(whole, whole),
        scratch_shapes=[pltpu.VMEM((4, part, lanes), BF)],
        compiler_params=limit,
    )(*pieces)
    return (
        input_grad.reshape(height, pairs * lanes),
        first.reshape(3, 3, channels, half),
        second.reshape(3, 3, half, mids).swapaxes(2, 3),
    )


def solution(mesh):
    return jax.shard_map(
        shards,
        mesh=mesh,
        in_specs=(
            P(("groups", "rows"), "tiles"),
            P(),
            P(),
            P(None, None, None, "chan"),
            P(("groups", "rows"), "tiles", "chan"),
            P(("groups", "rows"), "tiles"),
            P(("groups", "rows"), "tiles", None),
        ),
        out_specs=(
            P(("groups", "rows"), "tiles"),
            P("groups", None, None, "chan"),
            P("groups", None, None, "chan"),
        ),
        check_vma=False,
    )
```

```python
import functools
import math

import jax
import jax.numpy as jnp
from jax import lax
from jax.experimental import pallas as pl
from jax.experimental.pallas import tpu as pltpu
from jax.sharding import PartitionSpec as P

TP = 12
TISS_MEAN = 8
BF = jnp.bfloat16
F32 = jnp.float32
SLOTS = 64


def swaps(size, distance):
    return [(i, i ^ distance) for i in range(size) if (i ^ distance) < size]


def core_swapped(value):
    return lax.ppermute(value, "chan", [(0, 1), (1, 0)])


def shared_pairs(axis, n_tiles, n_rows):
    sizes = (n_tiles, n_rows)
    along = ("tiles", "rows").index(axis)
    size = sizes[along]
    pairs = []
    for t in range(n_tiles):
        for r in range(n_rows):
            for core in range(2):
                place, partner = [t, r], [t, r]
                if core == 0:
                    partner[along] = place[along] ^ 1
                else:
                    partner[along] = ((place[along] + 1) ^ 1) - 1
                if not 0 <= partner[along] < size:
                    partner[along] = place[along]
                    partner[1 - along] = place[1 - along] ^ 1
                    if partner[1 - along] >= sizes[1 - along]:
                        continue
                code = lambda p: (p[0] * n_rows + p[1]) * 2 + core
                pairs.append((code(place), code(partner)))
    return pairs


def sends_last(axis):
    even = lax.axis_index(axis) % 2 == 0
    return even if lax.axis_size(axis) <= 2 else (lax.axis_index("chan") == 0) == even


def traded(value, axis):
    size = lax.axis_size(axis)
    if size == 1:
        return jnp.zeros_like(value), jnp.zeros_like(value)
    if size == 2:
        got = lax.ppermute(value, axis, swaps(size, 1))
        return got, got
    pairs = shared_pairs(axis, lax.axis_size("tiles"), lax.axis_size("rows"))
    got = lax.ppermute(value, ("tiles", "rows", "chan"), pairs)
    return got, core_swapped(got)


def before_and_after(got, other, axis):
    index, none = lax.axis_index(axis), jnp.zeros_like(got)
    last = sends_last(axis)
    before = jnp.where(index == 0, none, jnp.where(last, other, got))
    after = jnp.where(index == lax.axis_size(axis) - 1, none, jnp.where(last, got, other))
    return before, after


def roll_columns(value, amount):
    return pltpu.roll(value, amount % SLOTS, axis=1)


def prepare_kernel(
    n_rows,
    order_hbm,
    cot_hbm,
    w1_hbm,
    w2_hbm,
    shift_hbm,
    near_ref,
    edge_ref,
    place_ref,
    w2_ref,
    wa_ref,
    shift_ref,
    cot,
    w1,
    order,
    rank,
    sems,
):
    rows, cols, half = cot.shape
    pairs = [
        (order_hbm, order),
        (cot_hbm, cot),
        (w1_hbm, w1),
        (w2_hbm, w2_ref),
        (shift_hbm, shift_ref),
    ]
    copies = [pltpu.make_async_copy(a, b, sems.at[i]) for i, (a, b) in enumerate(pairs)]
    for copy in copies:
        copy.start()
    copies[0].wait()
    for k in range(order.shape[2]):
        rank[order[0, 0, k]] = k
    side = TP // 2
    across = cols // side
    col_id = lax.broadcasted_iota(jnp.int32, (cols, 2 * half), 0)
    lane_id = lax.broadcasted_iota(jnp.int32, (cols, 2 * half), 1)
    mine = (lane_id < half) == (lax.axis_index("chan") == 0)
    for a in range(rows // side):
        place = jnp.zeros((cols, 2 * half), jnp.int32)
        for b in range(across):
            inside = (col_id >= b * side) & (col_id < (b + 1) * side)
            place = jnp.where(inside, rank[a * across + b], place)
        place_ref[a] = place
    copies[1].wait()
    lower = lax.axis_index("rows") % 2 == 0
    kept = []
    for i in range(rows):
        value = cot[i].astype(F32)
        placed = jnp.where(mine, jnp.concatenate([value, value], axis=1), 0.0)
        near_ref[i] = placed.astype(BF)
        kept.append(placed)
    for i in range(3):
        top, bottom = kept[i], kept[rows - 3 + i]
        at = slice(i * cols, (i + 1) * cols)
        if n_rows == 2:
            edge_ref[0, at, :] = jnp.where(lower, bottom, top).astype(BF)
        else:
            edge_ref[0, at, :] = top.astype(BF)
            edge_ref[1, at, :] = bottom.astype(BF)
    copies[2].wait()
    lanes = 2 * half
    for u in range(3):
        low = slice(u * lanes, u * lanes + half)
        high = slice(u * lanes + half, (u + 1) * lanes)
        wa_ref[low, :lanes] = jnp.zeros((half, lanes), BF)
        wa_ref[high, :lanes] = w1[u, 0]
        wa_ref[low, lanes:] = w1[u, 1]
        wa_ref[high, lanes:] = w1[u, 2]
    copies[3].wait()
    copies[4].wait()


def flat(value):
    return value.reshape(value.shape[0] * SLOTS, value.shape[2])


def image(value):
    return value.reshape(value.shape[0] // SLOTS, SLOTS, value.shape[1])


def block_place():
    return lax.axis_index("tiles") % 2 * 2 + lax.axis_index("rows") % 2


def main_kernel(
    n_tiles,
    n_rows,
    picture_ref,
    near_ref,
    far_ref,
    own_w2_ref,
    other_w2_ref,
    before_ref,
    after_ref,
    got_ref,
    got_other_ref,
    wa_ref,
    shift_ref,
    mid_ref,
    weight_ref,
    a_ref,
    u_ref,
    w2_ref,
):
    rows = u_ref.shape[0] - 6
    height, own_cols, lanes = picture_ref.shape
    tall = rows + 1
    half = lanes // 2
    row_index, tile_index = lax.axis_index("rows"), lax.axis_index("tiles")
    low = lax.axis_index("chan") == 0

    a_ref[0, :, :own_cols] = before_ref[:2]
    a_ref[rows + 1, :, :own_cols] = after_ref[:2]
    u_ref[:3, :own_cols] = before_ref[2:]
    u_ref[rows + 3 :, :own_cols] = after_ref[2:]
    for i in range(rows):
        a_ref[i + 1, :, :own_cols] = picture_ref[2 * i : 2 * i + 2]
        u_ref[i + 3, :own_cols] = near_ref[i] + far_ref[i]
    got, shared = got_ref[...].astype(F32), got_other_ref[...].astype(F32)
    mine_after = tile_index % 2 == 0
    if n_tiles > 2:
        mine_after = low == mine_after
        left_strip, right_strip = jnp.where(mine_after, shared, got), jnp.where(mine_after, got, shared)
    else:
        left_strip = right_strip = got
    left_strip = jnp.where(tile_index == 0, 0.0, left_strip)
    right_strip = jnp.where(tile_index == n_tiles - 1, 0.0, right_strip)

    def edge(at, count):
        fill = jnp.zeros((SLOTS - own_cols - 2 * count, lanes), F32)
        value = [right_strip[at : at + count], fill, left_strip[at : at + count]]
        return jnp.concatenate(value, axis=0).astype(BF)

    own_u, halo_a, halo_u = height, height + 4 * rows, height + 4 * rows + 4
    for i in range(height):
        a_ref[i // 2 + 1, i % 2, own_cols:] = edge(i, 1)
    for i in range(2):
        a_ref[0, i, own_cols:] = edge(halo_a + i, 1)
        a_ref[rows + 1, i, own_cols:] = edge(halo_a + 2 + i, 1)
    for i in range(rows):
        u_ref[i + 3, own_cols:] = edge(own_u + 4 * i, 4)
    for i in range(3):
        u_ref[i, own_cols:] = edge(halo_u + 4 * i, 4)
        u_ref[rows + 3 + i, own_cols:] = edge(halo_u + 12 + 4 * i, 4)

    def a_rows(count):
        return jnp.concatenate(
            [
                flat(a_ref[0:count, 1]),
                flat(a_ref[1 : count + 1, 0]),
                flat(a_ref[1 : count + 1, 1]),
            ],
            axis=1,
        )

    def u_rows(count):
        return jnp.concatenate([flat(u_ref[5 - 2 * u : 5 - 2 * u + count]) for u in range(3)], axis=1)

    for u in range(3):
        for w in range(3):
            at = slice((u * 3 + w) * half, (u * 3 + w + 1) * half)
            own_w, other_w = own_w2_ref[at, :], other_w2_ref[at, :]
            across = slice(w * lanes, (w + 1) * lanes)
            w2_ref[u * lanes : u * lanes + half, across] = jnp.where(low, own_w, other_w)
            w2_ref[u * lanes + half : (u + 1) * lanes, across] = jnp.where(low, other_w, own_w)

    row_id = lax.broadcasted_iota(jnp.int32, (tall, SLOTS, lanes), 0)
    col_id = lax.broadcasted_iota(jnp.int32, (tall, SLOTS, lanes), 1)
    own = (row_id < rows) & (col_id < own_cols)
    last_row = rows + jnp.where(row_index < n_rows - 1, 1, 0)
    last_col = own_cols + jnp.where(tile_index < n_tiles - 1, 1, 0)
    valid = (row_id < last_row) & (col_id < last_col)

    wa = wa_ref[...]
    part = jnp.dot(a_rows(tall), wa, preferred_element_type=F32)
    pre = image(part[:, lanes:]) + roll_columns(image(part[:, :lanes]), 1) + shift_ref[0]
    middle = jnp.maximum(pre, 0.0).astype(BF).astype(F32)

    mid_part = jnp.dot(u_rows(tall), w2_ref[...], preferred_element_type=F32)
    mid_raw = (
        roll_columns(image(mid_part[:, :lanes]), -2)
        + image(mid_part[:, lanes : 2 * lanes])
        + roll_columns(image(mid_part[:, 2 * lanes :]), 2)
    )
    mid_grad = jnp.where((middle > 0) & valid, mid_raw, 0.0)
    mid_ref[...] = mid_grad.astype(BF)

    middle_own = jnp.where(own, middle, 0.0)[:rows]
    middle_taps = jnp.concatenate(
        [
            flat(roll_columns(middle_own, 2)).astype(BF),
            flat(middle_own).astype(BF),
            flat(roll_columns(middle_own, -2)).astype(BF),
        ],
        axis=1,
    )
    over_pixels = (((0,), (0,)), ((), ()))
    second = lax.dot_general(u_rows(rows), middle_taps, over_pixels, preferred_element_type=F32)

    grad_own = jnp.where(own, mid_grad, 0.0)[:rows]
    grad_taps = jnp.concatenate(
        [flat(roll_columns(grad_own, -1)).astype(BF), flat(grad_own).astype(BF)], axis=1
    )
    first = lax.dot_general(a_rows(rows), grad_taps, over_pixels, preferred_element_type=F32)

    left = lax.broadcasted_iota(jnp.int32, (half, lanes), 1) < half

    part = weight_ref.shape[1]
    me = block_place()

    def keep(block, value):
        done = 0
        while done < half:
            number, at = divmod(block * half + done, part)
            count = min(part - at, half - done)
            weight_ref[number ^ me, at : at + count, :] = value[done : done + count].astype(BF)
            done += count

    def at_left(value):
        return jnp.where(low, value, pltpu.roll(value, half, axis=1))

    def at_right(value):
        return jnp.where(low, pltpu.roll(value, half, axis=1), value)

    centre = []
    for u in range(3):
        top = u * lanes
        for w in range(3):
            across = slice(w * lanes, (w + 1) * lanes)
            keep(
                u * 3 + w,
                jnp.where(low, second[top : top + half, across], second[top + half : top + lanes, across]),
            )
        outer = first[top + half : top + lanes]
        keep(9 + u, jnp.where(left, at_left(outer[:, :lanes]), at_right(outer[:, lanes:])))
        centre.append(first[top : top + half, lanes:])
    keep(12, jnp.where(left, at_left(centre[0]), at_right(centre[1])))
    keep(13, at_left(centre[2]))


def input_kernel(mid_ref, wa_ref, grad_ref):
    rows, own_cols, lanes = grad_ref.shape[0], grad_ref.shape[2], grad_ref.shape[3]
    tall = rows + 1
    by_lanes = (((1,), (1,)), ((), ()))
    grads = flat(mid_ref[...])
    wa = wa_ref[...]
    straight = lax.dot_general(grads, wa[:, lanes:], by_lanes, preferred_element_type=F32)
    shifted = lax.dot_general(grads, wa[:, :lanes], by_lanes, preferred_element_type=F32)

    def taps(u):
        s = slice(u * lanes, (u + 1) * lanes)
        return image(straight[:, s]) + roll_columns(image(shifted[:, s]), -1)

    above, level, below = taps(0), taps(1), taps(2)
    grad_ref[:, 0] = level[:rows, :own_cols].astype(BF)
    grad_ref[:, 1] = (below[:rows, :own_cols] + above[1:tall, :own_cols]).astype(BF)


def unpack_kernel(scale, piece_0, piece_1, piece_2, piece_3, first_ref, second_ref, all_ref):
    half = first_ref.shape[2]
    part = piece_0.shape[0]
    me = block_place()
    for distance, piece in enumerate((piece_0, piece_1, piece_2, piece_3)):
        all_ref[me ^ distance] = piece[...]

    def block(number):
        done, values = 0, []
        while done < half:
            which, at = divmod(number * half + done, part)
            count = min(part - at, half - done)
            values.append(all_ref[which, at : at + count, :].astype(F32) * scale)
            done += count
        return values[0] if len(values) == 1 else jnp.concatenate(values, axis=0)

    for tap in range(9):
        second_ref[tap] = block(tap)
    for u in range(3):
        value = block(9 + u)
        first_ref[3 * u] = value[:, :half]
        first_ref[3 * u + 2] = value[:, half:]
    value = block(12)
    first_ref[1] = value[:, :half]
    first_ref[4] = value[:, half:]
    first_ref[7] = block(13)[:, :half]


def summed_pair(value, axis, size, distance):
    got = lax.ppermute(value, axis, swaps(size, distance))
    return (value.astype(F32) + got.astype(F32)).astype(BF)


def shards(acts, shift, weight_one, weight_two, cotangent, tissue_count, tile_order):
    channels, mids = weight_one.shape[2], weight_one.shape[3]
    height = acts.shape[0]
    lanes = 2 * channels
    pairs = acts.shape[1] // lanes
    rows, cols = height // 2, pairs
    tile_rows, tile_cols = height // TP, 2 * pairs // TP
    out_side = TP // 2
    n_rows, n_tiles = lax.axis_size("rows"), lax.axis_size("tiles")

    whole = pl.BlockSpec(memory_space=pltpu.VMEM)
    in_hbm = pl.BlockSpec(memory_space=pltpu.HBM)
    limit = pltpu.CompilerParams(vmem_limit_bytes=48 << 20)
    half = channels
    n_edges = 1 if n_rows == 2 else 2
    near, edges, place, own_w2, wa, shift_row = pl.pallas_call(
        functools.partial(prepare_kernel, n_rows),
        out_shape=(
            jax.ShapeDtypeStruct((rows, cols, lanes), BF),
            jax.ShapeDtypeStruct((n_edges, 3 * cols, lanes), BF),
            jax.ShapeDtypeStruct((tile_rows, cols, lanes), jnp.int32),
            jax.ShapeDtypeStruct((9 * half, mids), BF),
            jax.ShapeDtypeStruct((3 * lanes, 2 * mids), BF),
            jax.ShapeDtypeStruct((1, mids), F32),
        ),
        in_specs=[in_hbm] * 5,
        out_specs=(whole,) * 6,
        scratch_shapes=[
            pltpu.VMEM((rows, cols, half), BF),
            pltpu.VMEM((3, 3, channels, mids), BF),
            pltpu.SMEM((1, 1, tile_rows * tile_cols), jnp.int32),
            pltpu.SMEM((tile_rows * tile_cols,), jnp.int32),
            pltpu.SemaphoreType.DMA((5,)),
        ],
        compiler_params=limit,
    )(
        *(
            pltpu.with_memory_space_constraint(value, pltpu.HBM)
            for value in (
                tile_order,
                cotangent,
                weight_one,
                weight_two.swapaxes(2, 3).reshape(9 * half, mids),
                shift.reshape(1, mids),
            )
        ),
    )
    other_edges = core_swapped(edges)
    edges, tissue_count = lax.optimization_barrier((edges, tissue_count))
    live = place < tissue_count[0, 0]
    near = jnp.where(live[:, None], near.reshape(tile_rows, -1, cols, lanes), jnp.zeros((), BF))
    near = near.reshape(rows, cols, lanes)
    edges = (edges + other_edges).reshape(n_edges, 3, cols, lanes)
    last = sends_last("rows")
    edge_u = edges[0] if n_rows == 2 else jnp.where(last, edges[1], edges[0])
    edge_u = jnp.where(jnp.where(last, live[-1], live[0]), edge_u, jnp.zeros((), BF))
    edge_u = edge_u.reshape(3 * cols, lanes)
    picture = acts.reshape(height, pairs, lanes)
    edge_a = jnp.where(last, picture[height - 2 :], picture[:2])
    strip = jnp.concatenate([edge_a.reshape(2 * cols, lanes), edge_u], axis=0)
    strip, near = lax.optimization_barrier((strip, near))
    before, after = (
        value.reshape(5, cols, lanes)
        for value in before_and_after(*traded(strip, "rows"), "rows")
    )
    far = core_swapped(near)
    own_w2, before = lax.optimization_barrier((own_w2, before))
    other_w2 = core_swapped(own_w2)

    right = sends_last("tiles")
    side = lambda value, count: jnp.where(
        right, value[:, cols - count :], value[:, :count]
    ).reshape(count * value.shape[0], lanes)
    got, got_other = traded(
        jnp.concatenate(
            [
                side(picture, 1),
                side(near, 4) + side(far, 4),
                side(before[:2], 1),
                side(after[:2], 1),
                side(before[2:], 4),
                side(after[2:], 4),
            ],
            axis=0,
        ),
        "tiles",
    )

    part = 14 * half // 4
    mid_grad, weights = pl.pallas_call(
        functools.partial(main_kernel, n_tiles, n_rows),
        out_shape=(
            jax.ShapeDtypeStruct((rows + 1, SLOTS, lanes), BF),
            jax.ShapeDtypeStruct((4, part, lanes), BF),
        ),
        in_specs=[whole] * 11,
        out_specs=(whole, whole),
        scratch_shapes=[
            pltpu.VMEM((rows + 2, 2, SLOTS, lanes), BF),
            pltpu.VMEM((rows + 6, SLOTS, lanes), BF),
            pltpu.VMEM((3 * lanes, 3 * mids), BF),
        ],
        compiler_params=limit,
    )(picture, near, far, own_w2, other_w2, before, after, got, got_other, wa, shift_row)
    input_grad = pl.pallas_call(
        input_kernel,
        out_shape=jax.ShapeDtypeStruct((rows, 2, cols, lanes), BF),
        in_specs=[whole, whole],
        out_specs=whole,
        compiler_params=limit,
    )(mid_grad, wa)

    def from_block(values):
        got = {}
        for d in (1, 2, 3):
            value = values[d - 1]
            for other in got.values():
                value, _ = lax.optimization_barrier((value, other[0]))
            pairs = [
                (t * n_rows + r, (t ^ (d >> 1)) * n_rows + (r ^ (d & 1)))
                for t in range(n_tiles)
                for r in range(n_rows)
            ]
            got[d] = (value, lax.ppermute(value, ("tiles", "rows"), pairs))
        return [got[d][1] for d in (1, 2, 3)]

    one, two, three = from_block([weights[1], weights[2], weights[3]])
    total = (
        (weights[0].astype(F32) + one.astype(F32)) + (two.astype(F32) + three.astype(F32))
    ).astype(BF)
    distance = 2
    while distance < n_rows:
        total = summed_pair(total, "rows", n_rows, distance)
        distance *= 2
    distance = 2
    while distance < n_tiles:
        total = summed_pair(total, "tiles", n_tiles, distance)
        distance *= 2
    pieces = [total] + from_block([total] * 3)

    pixels = n_rows * TISS_MEAN * n_tiles * out_side * out_side
    scale = 1.0 / math.sqrt(pixels)
    first, second = pl.pallas_call(
        functools.partial(unpack_kernel, scale),
        out_shape=(
            jax.ShapeDtypeStruct((9, channels, half), F32),
            jax.ShapeDtypeStruct((9, half, mids), F32),
        ),
        in_specs=[whole] * 4,
        out_specs=(whole, whole),
        scratch_shapes=[pltpu.VMEM((4, part, lanes), BF)],
        compiler_params=limit,
    )(*pieces)
    return (
        input_grad.reshape(height, pairs * lanes),
        first.reshape(3, 3, channels, half),
        second.reshape(3, 3, half, mids).swapaxes(2, 3),
    )


def solution(mesh):
    return jax.shard_map(
        shards,
        mesh=mesh,
        in_specs=(
            P(("groups", "rows"), "tiles"),
            P(),
            P(),
            P(None, None, None, "chan"),
            P(("groups", "rows"), "tiles", "chan"),
            P(("groups", "rows"), "tiles"),
            P(("groups", "rows"), "tiles", None),
        ),
        out_specs=(
            P(("groups", "rows"), "tiles"),
            P("groups", None, None, "chan"),
            P("groups", None, None, "chan"),
        ),
        check_vma=False,
    )
```

```python
import functools
import math

import jax
import jax.numpy as jnp
from jax import lax
from jax.experimental import pallas as pl
from jax.experimental.pallas import tpu as pltpu
from jax.sharding import PartitionSpec as P

TP = 12
TISS_MEAN = 8
BF = jnp.bfloat16
F32 = jnp.float32
SLOTS = 64


def swaps(size, distance):
    return [(i, i ^ distance) for i in range(size) if (i ^ distance) < size]


def core_swapped(value):
    return lax.ppermute(value, "chan", [(0, 1), (1, 0)])


def shared_pairs(axis, n_tiles, n_rows):
    sizes = (n_tiles, n_rows)
    along = ("tiles", "rows").index(axis)
    size = sizes[along]
    pairs = []
    for t in range(n_tiles):
        for r in range(n_rows):
            for core in range(2):
                place, partner = [t, r], [t, r]
                if core == 0:
                    partner[along] = place[along] ^ 1
                else:
                    partner[along] = ((place[along] + 1) ^ 1) - 1
                if not 0 <= partner[along] < size:
                    partner[along] = place[along]
                    partner[1 - along] = place[1 - along] ^ 1
                    if partner[1 - along] >= sizes[1 - along]:
                        continue
                code = lambda p: (p[0] * n_rows + p[1]) * 2 + core
                pairs.append((code(place), code(partner)))
    return pairs


def sends_last(axis):
    even = lax.axis_index(axis) % 2 == 0
    return even if lax.axis_size(axis) <= 2 else (lax.axis_index("chan") == 0) == even


def traded(value, axis):
    size = lax.axis_size(axis)
    if size == 1:
        return jnp.zeros_like(value), jnp.zeros_like(value)
    if size == 2:
        got = lax.ppermute(value, axis, swaps(size, 1))
        return got, got
    pairs = shared_pairs(axis, lax.axis_size("tiles"), lax.axis_size("rows"))
    got = lax.ppermute(value, ("tiles", "rows", "chan"), pairs)
    return got, core_swapped(got)


def before_and_after(got, other, axis):
    index, none = lax.axis_index(axis), jnp.zeros_like(got)
    last = sends_last(axis)
    before = jnp.where(index == 0, none, jnp.where(last, other, got))
    after = jnp.where(index == lax.axis_size(axis) - 1, none, jnp.where(last, got, other))
    return before, after


def roll_columns(value, amount):
    return pltpu.roll(value, amount % SLOTS, axis=1)


def prepare_kernel(
    n_rows,
    order_hbm,
    cot_hbm,
    w1_hbm,
    w2_hbm,
    shift_hbm,
    near_ref,
    edge_ref,
    place_ref,
    w2_ref,
    wa_ref,
    shift_ref,
    cot,
    w1,
    order,
    rank,
    sems,
):
    rows, cols, half = cot.shape
    pairs = [
        (order_hbm, order),
        (cot_hbm, cot),
        (w1_hbm, w1),
        (w2_hbm, w2_ref),
        (shift_hbm, shift_ref),
    ]
    copies = [pltpu.make_async_copy(a, b, sems.at[i]) for i, (a, b) in enumerate(pairs)]
    for copy in copies:
        copy.start()
    copies[0].wait()
    for k in range(order.shape[2]):
        rank[order[0, 0, k]] = k
    side = TP // 2
    across = cols // side
    col_id = lax.broadcasted_iota(jnp.int32, (cols, 2 * half), 0)
    lane_id = lax.broadcasted_iota(jnp.int32, (cols, 2 * half), 1)
    mine = (lane_id < half) == (lax.axis_index("chan") == 0)
    for a in range(rows // side):
        place = jnp.zeros((cols, 2 * half), jnp.int32)
        for b in range(across):
            inside = (col_id >= b * side) & (col_id < (b + 1) * side)
            place = jnp.where(inside, rank[a * across + b], place)
        place_ref[a] = place
    copies[1].wait()
    lower = lax.axis_index("rows") % 2 == 0
    kept = []
    for i in range(rows):
        value = cot[i].astype(F32)
        placed = jnp.where(mine, jnp.concatenate([value, value], axis=1), 0.0)
        near_ref[i] = placed.astype(BF)
        kept.append(placed)
    for i in range(3):
        top, bottom = kept[i], kept[rows - 3 + i]
        at = slice(i * cols, (i + 1) * cols)
        if n_rows == 2:
            edge_ref[0, at, :] = jnp.where(lower, bottom, top).astype(BF)
        else:
            edge_ref[0, at, :] = top.astype(BF)
            edge_ref[1, at, :] = bottom.astype(BF)
    copies[2].wait()
    lanes = 2 * half
    for u in range(3):
        low = slice(u * lanes, u * lanes + half)
        high = slice(u * lanes + half, (u + 1) * lanes)
        wa_ref[low, :lanes] = jnp.zeros((half, lanes), BF)
        wa_ref[high, :lanes] = w1[u, 0]
        wa_ref[low, lanes:] = w1[u, 1]
        wa_ref[high, lanes:] = w1[u, 2]
    copies[3].wait()
    copies[4].wait()


def flat(value):
    return value.reshape(value.shape[0] * SLOTS, value.shape[2])


def image(value):
    return value.reshape(value.shape[0] // SLOTS, SLOTS, value.shape[1])


def block_place():
    return lax.axis_index("tiles") % 2 * 2 + lax.axis_index("rows") % 2


def main_kernel(
    n_tiles,
    n_rows,
    picture_ref,
    near_ref,
    far_ref,
    own_w2_ref,
    other_w2_ref,
    before_ref,
    after_ref,
    got_ref,
    got_other_ref,
    wa_ref,
    shift_ref,
    mid_ref,
    weight_ref,
    a_ref,
    u_ref,
    w2_ref,
):
    rows = u_ref.shape[0] - 6
    height, own_cols, lanes = picture_ref.shape
    tall = rows + 1
    half = lanes // 2
    row_index, tile_index = lax.axis_index("rows"), lax.axis_index("tiles")
    low = lax.axis_index("chan") == 0

    a_ref[0, :, :own_cols] = before_ref[:2]
    a_ref[rows + 1, :, :own_cols] = after_ref[:2]
    u_ref[:3, :own_cols] = before_ref[2:]
    u_ref[rows + 3 :, :own_cols] = after_ref[2:]
    for i in range(rows):
        a_ref[i + 1, :, :own_cols] = picture_ref[2 * i : 2 * i + 2]
        u_ref[i + 3, :own_cols] = near_ref[i] + far_ref[i]
    got, shared = got_ref[...].astype(F32), got_other_ref[...].astype(F32)
    mine_after = tile_index % 2 == 0
    if n_tiles > 2:
        mine_after = low == mine_after
        left_strip, right_strip = jnp.where(mine_after, shared, got), jnp.where(mine_after, got, shared)
    else:
        left_strip = right_strip = got
    left_strip = jnp.where(tile_index == 0, 0.0, left_strip)
    right_strip = jnp.where(tile_index == n_tiles - 1, 0.0, right_strip)

    def edge(at, count):
        fill = jnp.zeros((SLOTS - own_cols - 2 * count, lanes), F32)
        value = [right_strip[at : at + count], fill, left_strip[at : at + count]]
        return jnp.concatenate(value, axis=0).astype(BF)

    own_u, halo_a, halo_u = height, height + 4 * rows, height + 4 * rows + 4
    for i in range(height):
        a_ref[i // 2 + 1, i % 2, own_cols:] = edge(i, 1)
    for i in range(2):
        a_ref[0, i, own_cols:] = edge(halo_a + i, 1)
        a_ref[rows + 1, i, own_cols:] = edge(halo_a + 2 + i, 1)
    for i in range(rows):
        u_ref[i + 3, own_cols:] = edge(own_u + 4 * i, 4)
    for i in range(3):
        u_ref[i, own_cols:] = edge(halo_u + 4 * i, 4)
        u_ref[rows + 3 + i, own_cols:] = edge(halo_u + 12 + 4 * i, 4)

    def a_rows(count):
        return jnp.concatenate(
            [
                flat(a_ref[0:count, 1]),
                flat(a_ref[1 : count + 1, 0]),
                flat(a_ref[1 : count + 1, 1]),
            ],
            axis=1,
        )

    def u_rows(count):
        return jnp.concatenate([flat(u_ref[5 - 2 * u : 5 - 2 * u + count]) for u in range(3)], axis=1)

    for u in range(3):
        for w in range(3):
            at = slice((u * 3 + w) * half, (u * 3 + w + 1) * half)
            own_w, other_w = own_w2_ref[at, :], other_w2_ref[at, :]
            across = slice(w * lanes, (w + 1) * lanes)
            w2_ref[u * lanes : u * lanes + half, across] = jnp.where(low, own_w, other_w)
            w2_ref[u * lanes + half : (u + 1) * lanes, across] = jnp.where(low, other_w, own_w)

    row_id = lax.broadcasted_iota(jnp.int32, (tall, SLOTS, lanes), 0)
    col_id = lax.broadcasted_iota(jnp.int32, (tall, SLOTS, lanes), 1)
    own = (row_id < rows) & (col_id < own_cols)
    last_row = rows + jnp.where(row_index < n_rows - 1, 1, 0)
    last_col = own_cols + jnp.where(tile_index < n_tiles - 1, 1, 0)
    valid = (row_id < last_row) & (col_id < last_col)

    wa = wa_ref[...]
    part = jnp.dot(a_rows(tall), wa, preferred_element_type=F32)
    pre = image(part[:, lanes:]) + roll_columns(image(part[:, :lanes]), 1) + shift_ref[0]
    middle = jnp.maximum(pre, 0.0).astype(BF).astype(F32)

    mid_part = jnp.dot(u_rows(tall), w2_ref[...], preferred_element_type=F32)
    mid_raw = (
        roll_columns(image(mid_part[:, :lanes]), -2)
        + image(mid_part[:, lanes : 2 * lanes])
        + roll_columns(image(mid_part[:, 2 * lanes :]), 2)
    )
    mid_grad = jnp.where((middle > 0) & valid, mid_raw, 0.0)
    mid_ref[...] = mid_grad.astype(BF)

    middle_own = jnp.where(own, middle, 0.0)[:rows]
    middle_taps = jnp.concatenate(
        [
            flat(roll_columns(middle_own, 2)).astype(BF),
            flat(middle_own).astype(BF),
            flat(roll_columns(middle_own, -2)).astype(BF),
        ],
        axis=1,
    )
    over_pixels = (((0,), (0,)), ((), ()))
    second = lax.dot_general(u_rows(rows), middle_taps, over_pixels, preferred_element_type=F32)

    grad_own = jnp.where(own, mid_grad, 0.0)[:rows]
    grad_taps = jnp.concatenate(
        [flat(roll_columns(grad_own, -1)).astype(BF), flat(grad_own).astype(BF)], axis=1
    )
    first = lax.dot_general(a_rows(rows), grad_taps, over_pixels, preferred_element_type=F32)

    left = lax.broadcasted_iota(jnp.int32, (half, lanes), 1) < half

    part = weight_ref.shape[1]
    me = block_place()

    def keep(block, value):
        done = 0
        while done < half:
            number, at = divmod(block * half + done, part)
            count = min(part - at, half - done)
            weight_ref[number ^ me, at : at + count, :] = value[done : done + count].astype(BF)
            done += count

    def at_left(value):
        return jnp.where(low, value, pltpu.roll(value, half, axis=1))

    def at_right(value):
        return jnp.where(low, pltpu.roll(value, half, axis=1), value)

    centre = []
    for u in range(3):
        top = u * lanes
        for w in range(3):
            across = slice(w * lanes, (w + 1) * lanes)
            keep(
                u * 3 + w,
                jnp.where(low, second[top : top + half, across], second[top + half : top + lanes, across]),
            )
        outer = first[top + half : top + lanes]
        keep(9 + u, jnp.where(left, at_left(outer[:, :lanes]), at_right(outer[:, lanes:])))
        centre.append(first[top : top + half, lanes:])
    keep(12, jnp.where(left, at_left(centre[0]), at_right(centre[1])))
    keep(13, at_left(centre[2]))


def input_kernel(mid_ref, wa_ref, grad_ref):
    rows, own_cols, lanes = grad_ref.shape[0], grad_ref.shape[2], grad_ref.shape[3]
    tall = rows + 1
    by_lanes = (((1,), (1,)), ((), ()))
    grads = flat(mid_ref[...])
    wa = wa_ref[...]
    straight = lax.dot_general(grads, wa[:, lanes:], by_lanes, preferred_element_type=F32)
    shifted = lax.dot_general(grads, wa[:, :lanes], by_lanes, preferred_element_type=F32)

    def taps(u):
        s = slice(u * lanes, (u + 1) * lanes)
        return image(straight[:, s]) + roll_columns(image(shifted[:, s]), -1)

    above, level, below = taps(0), taps(1), taps(2)
    grad_ref[:, 0] = level[:rows, :own_cols].astype(BF)
    grad_ref[:, 1] = (below[:rows, :own_cols] + above[1:tall, :own_cols]).astype(BF)


def unpack_kernel(scale, piece_0, piece_1, piece_2, piece_3, first_ref, second_ref, all_ref):
    half = first_ref.shape[2]
    part = piece_0.shape[0]
    me = block_place()
    for distance, piece in enumerate((piece_0, piece_1, piece_2, piece_3)):
        all_ref[me ^ distance] = piece[...]

    def block(number):
        done, values = 0, []
        while done < half:
            which, at = divmod(number * half + done, part)
            count = min(part - at, half - done)
            values.append(all_ref[which, at : at + count, :].astype(F32) * scale)
            done += count
        return values[0] if len(values) == 1 else jnp.concatenate(values, axis=0)

    for tap in range(9):
        second_ref[tap] = block(tap)
    for u in range(3):
        value = block(9 + u)
        first_ref[3 * u] = value[:, :half]
        first_ref[3 * u + 2] = value[:, half:]
    value = block(12)
    first_ref[1] = value[:, :half]
    first_ref[4] = value[:, half:]
    first_ref[7] = block(13)[:, :half]


def summed_pair(value, axis, size, distance):
    got = lax.ppermute(value, axis, swaps(size, distance))
    return (value.astype(F32) + got.astype(F32)).astype(BF)


def shards(acts, shift, weight_one, weight_two, cotangent, tissue_count, tile_order):
    channels, mids = weight_one.shape[2], weight_one.shape[3]
    height = acts.shape[0]
    lanes = 2 * channels
    pairs = acts.shape[1] // lanes
    rows, cols = height // 2, pairs
    tile_rows, tile_cols = height // TP, 2 * pairs // TP
    out_side = TP // 2
    n_rows, n_tiles = lax.axis_size("rows"), lax.axis_size("tiles")

    whole = pl.BlockSpec(memory_space=pltpu.VMEM)
    in_hbm = pl.BlockSpec(memory_space=pltpu.HBM)
    limit = pltpu.CompilerParams(vmem_limit_bytes=48 << 20)
    half = channels
    n_edges = 1 if n_rows == 2 else 2
    near, edges, place, own_w2, wa, shift_row = pl.pallas_call(
        functools.partial(prepare_kernel, n_rows),
        out_shape=(
            jax.ShapeDtypeStruct((rows, cols, lanes), BF),
            jax.ShapeDtypeStruct((n_edges, 3 * cols, lanes), BF),
            jax.ShapeDtypeStruct((tile_rows, cols, lanes), jnp.int32),
            jax.ShapeDtypeStruct((9 * half, mids), BF),
            jax.ShapeDtypeStruct((3 * lanes, 2 * mids), BF),
            jax.ShapeDtypeStruct((1, mids), F32),
        ),
        in_specs=[in_hbm] * 5,
        out_specs=(whole,) * 6,
        scratch_shapes=[
            pltpu.VMEM((rows, cols, half), BF),
            pltpu.VMEM((3, 3, channels, mids), BF),
            pltpu.SMEM((1, 1, tile_rows * tile_cols), jnp.int32),
            pltpu.SMEM((tile_rows * tile_cols,), jnp.int32),
            pltpu.SemaphoreType.DMA((5,)),
        ],
        compiler_params=limit,
    )(
        *(
            pltpu.with_memory_space_constraint(value, pltpu.HBM)
            for value in (
                tile_order,
                cotangent,
                weight_one,
                weight_two.swapaxes(2, 3).reshape(9 * half, mids),
                shift.reshape(1, mids),
            )
        ),
    )
    other_edges = core_swapped(edges)
    edges, tissue_count = lax.optimization_barrier((edges, tissue_count))
    live = place < tissue_count[0, 0]
    near = jnp.where(live[:, None], near.reshape(tile_rows, -1, cols, lanes), jnp.zeros((), BF))
    near = near.reshape(rows, cols, lanes)
    edges = (edges + other_edges).reshape(n_edges, 3, cols, lanes)
    last = sends_last("rows")
    edge_u = edges[0] if n_rows == 2 else jnp.where(last, edges[1], edges[0])
    edge_u = jnp.where(jnp.where(last, live[-1], live[0]), edge_u, jnp.zeros((), BF))
    edge_u = edge_u.reshape(3 * cols, lanes)
    picture = acts.reshape(height, pairs, lanes)
    edge_a = jnp.where(last, picture[height - 2 :], picture[:2])
    strip = jnp.concatenate([edge_a.reshape(2 * cols, lanes), edge_u], axis=0)
    strip, near, own_w2 = lax.optimization_barrier((strip, near, own_w2))
    before, after = (
        value.reshape(5, cols, lanes)
        for value in before_and_after(*traded(strip, "rows"), "rows")
    )
    far = core_swapped(near)
    other_w2 = core_swapped(own_w2)

    right = sends_last("tiles")
    side = lambda value, count: jnp.where(
        right, value[:, cols - count :], value[:, :count]
    ).reshape(count * value.shape[0], lanes)
    got, got_other = traded(
        jnp.concatenate(
            [
                side(picture, 1),
                side(near, 4) + side(far, 4),
                side(before[:2], 1),
                side(after[:2], 1),
                side(before[2:], 4),
                side(after[2:], 4),
            ],
            axis=0,
        ),
        "tiles",
    )

    part = 14 * half // 4
    mid_grad, weights = pl.pallas_call(
        functools.partial(main_kernel, n_tiles, n_rows),
        out_shape=(
            jax.ShapeDtypeStruct((rows + 1, SLOTS, lanes), BF),
            jax.ShapeDtypeStruct((4, part, lanes), BF),
        ),
        in_specs=[whole] * 11,
        out_specs=(whole, whole),
        scratch_shapes=[
            pltpu.VMEM((rows + 2, 2, SLOTS, lanes), BF),
            pltpu.VMEM((rows + 6, SLOTS, lanes), BF),
            pltpu.VMEM((3 * lanes, 3 * mids), BF),
        ],
        compiler_params=limit,
    )(picture, near, far, own_w2, other_w2, before, after, got, got_other, wa, shift_row)
    input_grad = pl.pallas_call(
        input_kernel,
        out_shape=jax.ShapeDtypeStruct((rows, 2, cols, lanes), BF),
        in_specs=[whole, whole],
        out_specs=whole,
        compiler_params=limit,
    )(mid_grad, wa)

    def from_block(values):
        got = {}
        for d in (1, 2, 3):
            value = values[d - 1]
            for other in got.values():
                value, _ = lax.optimization_barrier((value, other[0]))
            pairs = [
                (t * n_rows + r, (t ^ (d >> 1)) * n_rows + (r ^ (d & 1)))
                for t in range(n_tiles)
                for r in range(n_rows)
            ]
            got[d] = (value, lax.ppermute(value, ("tiles", "rows"), pairs))
        return [got[d][1] for d in (1, 2, 3)]

    one, two, three = from_block([weights[1], weights[2], weights[3]])
    total = (
        (weights[0].astype(F32) + one.astype(F32)) + (two.astype(F32) + three.astype(F32))
    ).astype(BF)
    distance = 2
    while distance < n_rows:
        total = summed_pair(total, "rows", n_rows, distance)
        distance *= 2
    distance = 2
    while distance < n_tiles:
        total = summed_pair(total, "tiles", n_tiles, distance)
        distance *= 2
    pieces = [total] + from_block([total] * 3)

    pixels = n_rows * TISS_MEAN * n_tiles * out_side * out_side
    scale = 1.0 / math.sqrt(pixels)
    first, second = pl.pallas_call(
        functools.partial(unpack_kernel, scale),
        out_shape=(
            jax.ShapeDtypeStruct((9, channels, half), F32),
            jax.ShapeDtypeStruct((9, half, mids), F32),
        ),
        in_specs=[whole] * 4,
        out_specs=(whole, whole),
        scratch_shapes=[pltpu.VMEM((4, part, lanes), BF)],
        compiler_params=limit,
    )(*pieces)
    return (
        input_grad.reshape(height, pairs * lanes),
        first.reshape(3, 3, channels, half),
        second.reshape(3, 3, half, mids).swapaxes(2, 3),
    )


def solution(mesh):
    return jax.shard_map(
        shards,
        mesh=mesh,
        in_specs=(
            P(("groups", "rows"), "tiles"),
            P(),
            P(),
            P(None, None, None, "chan"),
            P(("groups", "rows"), "tiles", "chan"),
            P(("groups", "rows"), "tiles"),
            P(("groups", "rows"), "tiles", None),
        ),
        out_specs=(
            P(("groups", "rows"), "tiles"),
            P("groups", None, None, "chan"),
            P("groups", None, None, "chan"),
        ),
        check_vma=False,
    )
```

```python
import functools
import math

import jax
import jax.numpy as jnp
from jax import lax
from jax.experimental import pallas as pl
from jax.experimental.pallas import tpu as pltpu
from jax.sharding import PartitionSpec as P

TP = 12
TISS_MEAN = 8
BF = jnp.bfloat16
F32 = jnp.float32
SLOTS = 64


def swaps(size, distance):
    return [(i, i ^ distance) for i in range(size) if (i ^ distance) < size]


def core_swapped(value):
    return lax.ppermute(value, "chan", [(0, 1), (1, 0)])


def shared_pairs(axis, n_tiles, n_rows):
    sizes = (n_tiles, n_rows)
    along = ("tiles", "rows").index(axis)
    size = sizes[along]
    pairs = []
    for t in range(n_tiles):
        for r in range(n_rows):
            for core in range(2):
                place, partner = [t, r], [t, r]
                if core == 0:
                    partner[along] = place[along] ^ 1
                else:
                    partner[along] = ((place[along] + 1) ^ 1) - 1
                if not 0 <= partner[along] < size:
                    partner[along] = place[along]
                    partner[1 - along] = place[1 - along] ^ 1
                    if partner[1 - along] >= sizes[1 - along]:
                        continue
                code = lambda p: (p[0] * n_rows + p[1]) * 2 + core
                pairs.append((code(place), code(partner)))
    return pairs


def sends_last(axis):
    even = lax.axis_index(axis) % 2 == 0
    return even if lax.axis_size(axis) <= 2 else (lax.axis_index("chan") == 0) == even


def traded(value, axis):
    size = lax.axis_size(axis)
    if size == 1:
        return jnp.zeros_like(value), jnp.zeros_like(value)
    if size == 2:
        got = lax.ppermute(value, axis, swaps(size, 1))
        return got, got
    pairs = shared_pairs(axis, lax.axis_size("tiles"), lax.axis_size("rows"))
    got = lax.ppermute(value, ("tiles", "rows", "chan"), pairs)
    return got, core_swapped(got)


def before_and_after(got, other, axis):
    index, none = lax.axis_index(axis), jnp.zeros_like(got)
    last = sends_last(axis)
    before = jnp.where(index == 0, none, jnp.where(last, other, got))
    after = jnp.where(index == lax.axis_size(axis) - 1, none, jnp.where(last, got, other))
    return before, after


def roll_columns(value, amount):
    return pltpu.roll(value, amount % SLOTS, axis=1)


def prepare_kernel(
    n_rows,
    order_hbm,
    cot_hbm,
    w1_hbm,
    w2_hbm,
    shift_hbm,
    near_ref,
    edge_ref,
    place_ref,
    w2_ref,
    wa_ref,
    shift_ref,
    cot,
    w1,
    order,
    rank,
    sems,
):
    rows, cols, half = cot.shape
    pairs = [
        (order_hbm, order),
        (cot_hbm, cot),
        (w1_hbm, w1),
        (w2_hbm, w2_ref),
        (shift_hbm, shift_ref),
    ]
    copies = [pltpu.make_async_copy(a, b, sems.at[i]) for i, (a, b) in enumerate(pairs)]
    for copy in copies:
        copy.start()
    copies[0].wait()
    for k in range(order.shape[2]):
        rank[order[0, 0, k]] = k
    side = TP // 2
    across = cols // side
    col_id = lax.broadcasted_iota(jnp.int32, (cols, 2 * half), 0)
    lane_id = lax.broadcasted_iota(jnp.int32, (cols, 2 * half), 1)
    mine = (lane_id < half) == (lax.axis_index("chan") == 0)
    for a in range(rows // side):
        place = jnp.zeros((cols, 2 * half), jnp.int32)
        for b in range(across):
            inside = (col_id >= b * side) & (col_id < (b + 1) * side)
            place = jnp.where(inside, rank[a * across + b], place)
        place_ref[a] = place
    copies[1].wait()
    lower = lax.axis_index("rows") % 2 == 0
    kept = []
    for i in range(rows):
        value = cot[i].astype(F32)
        placed = jnp.where(mine, jnp.concatenate([value, value], axis=1), 0.0)
        near_ref[i] = placed.astype(BF)
        kept.append(placed)
    for i in range(3):
        top, bottom = kept[i], kept[rows - 3 + i]
        at = slice(i * cols, (i + 1) * cols)
        if n_rows == 2:
            edge_ref[0, at, :] = jnp.where(lower, bottom, top).astype(BF)
        else:
            edge_ref[0, at, :] = top.astype(BF)
            edge_ref[1, at, :] = bottom.astype(BF)
    copies[2].wait()
    lanes = 2 * half
    for u in range(3):
        low = slice(u * lanes, u * lanes + half)
        high = slice(u * lanes + half, (u + 1) * lanes)
        wa_ref[low, :lanes] = jnp.zeros((half, lanes), BF)
        wa_ref[high, :lanes] = w1[u, 0]
        wa_ref[low, lanes:] = w1[u, 1]
        wa_ref[high, lanes:] = w1[u, 2]
    copies[3].wait()
    copies[4].wait()


def flat(value):
    return value.reshape(value.shape[0] * SLOTS, value.shape[2])


def image(value):
    return value.reshape(value.shape[0] // SLOTS, SLOTS, value.shape[1])


def block_place():
    return lax.axis_index("tiles") % 2 * 2 + lax.axis_index("rows") % 2


def main_kernel(
    n_tiles,
    n_rows,
    picture_ref,
    near_ref,
    far_ref,
    own_w2_ref,
    other_w2_ref,
    before_ref,
    after_ref,
    got_ref,
    got_other_ref,
    wa_ref,
    shift_ref,
    mid_ref,
    weight_ref,
    a_ref,
    u_ref,
    w2_ref,
):
    rows = u_ref.shape[0] - 6
    height, own_cols, lanes = picture_ref.shape
    tall = rows + 1
    half = lanes // 2
    row_index, tile_index = lax.axis_index("rows"), lax.axis_index("tiles")
    low = lax.axis_index("chan") == 0

    a_ref[0, :, :own_cols] = before_ref[:2]
    a_ref[rows + 1, :, :own_cols] = after_ref[:2]
    u_ref[:3, :own_cols] = before_ref[2:]
    u_ref[rows + 3 :, :own_cols] = after_ref[2:]
    for i in range(rows):
        a_ref[i + 1, :, :own_cols] = picture_ref[2 * i : 2 * i + 2]
        u_ref[i + 3, :own_cols] = near_ref[i] + far_ref[i]
    got, shared = got_ref[...].astype(F32), got_other_ref[...].astype(F32)
    mine_after = tile_index % 2 == 0
    if n_tiles > 2:
        mine_after = low == mine_after
        left_strip, right_strip = jnp.where(mine_after, shared, got), jnp.where(mine_after, got, shared)
    else:
        left_strip = right_strip = got
    left_strip = jnp.where(tile_index == 0, 0.0, left_strip)
    right_strip = jnp.where(tile_index == n_tiles - 1, 0.0, right_strip)

    def edge(at, count):
        fill = jnp.zeros((SLOTS - own_cols - 2 * count, lanes), F32)
        value = [right_strip[at : at + count], fill, left_strip[at : at + count]]
        return jnp.concatenate(value, axis=0).astype(BF)

    own_a, halo_a, halo_u = 4 * rows, height + 4 * rows, height + 4 * rows + 4
    for i in range(height):
        a_ref[i // 2 + 1, i % 2, own_cols:] = edge(own_a + i, 1)
    for i in range(2):
        a_ref[0, i, own_cols:] = edge(halo_a + i, 1)
        a_ref[rows + 1, i, own_cols:] = edge(halo_a + 2 + i, 1)
    for i in range(rows):
        u_ref[i + 3, own_cols:] = edge(4 * i, 4)
    for i in range(3):
        u_ref[i, own_cols:] = edge(halo_u + 4 * i, 4)
        u_ref[rows + 3 + i, own_cols:] = edge(halo_u + 12 + 4 * i, 4)

    def a_rows(count):
        return jnp.concatenate(
            [
                flat(a_ref[0:count, 1]),
                flat(a_ref[1 : count + 1, 0]),
                flat(a_ref[1 : count + 1, 1]),
            ],
            axis=1,
        )

    def u_rows(count):
        return jnp.concatenate([flat(u_ref[5 - 2 * u : 5 - 2 * u + count]) for u in range(3)], axis=1)

    for u in range(3):
        for w in range(3):
            at = slice((u * 3 + w) * half, (u * 3 + w + 1) * half)
            own_w, other_w = own_w2_ref[at, :], other_w2_ref[at, :]
            across = slice(w * lanes, (w + 1) * lanes)
            w2_ref[u * lanes : u * lanes + half, across] = jnp.where(low, own_w, other_w)
            w2_ref[u * lanes + half : (u + 1) * lanes, across] = jnp.where(low, other_w, own_w)

    row_id = lax.broadcasted_iota(jnp.int32, (tall, SLOTS, lanes), 0)
    col_id = lax.broadcasted_iota(jnp.int32, (tall, SLOTS, lanes), 1)
    own = (row_id < rows) & (col_id < own_cols)
    last_row = rows + jnp.where(row_index < n_rows - 1, 1, 0)
    last_col = own_cols + jnp.where(tile_index < n_tiles - 1, 1, 0)
    valid = (row_id < last_row) & (col_id < last_col)

    wa = wa_ref[...]
    part = jnp.dot(a_rows(tall), wa, preferred_element_type=F32)
    pre = image(part[:, lanes:]) + roll_columns(image(part[:, :lanes]), 1) + shift_ref[0]
    middle = jnp.maximum(pre, 0.0).astype(BF).astype(F32)

    mid_part = jnp.dot(u_rows(tall), w2_ref[...], preferred_element_type=F32)
    mid_raw = (
        roll_columns(image(mid_part[:, :lanes]), -2)
        + image(mid_part[:, lanes : 2 * lanes])
        + roll_columns(image(mid_part[:, 2 * lanes :]), 2)
    )
    mid_grad = jnp.where((middle > 0) & valid, mid_raw, 0.0)
    mid_ref[...] = mid_grad.astype(BF)

    middle_own = jnp.where(own, middle, 0.0)[:rows]
    middle_taps = jnp.concatenate(
        [
            flat(roll_columns(middle_own, 2)).astype(BF),
            flat(middle_own).astype(BF),
            flat(roll_columns(middle_own, -2)).astype(BF),
        ],
        axis=1,
    )
    over_pixels = (((0,), (0,)), ((), ()))
    second = lax.dot_general(u_rows(rows), middle_taps, over_pixels, preferred_element_type=F32)

    grad_own = jnp.where(own, mid_grad, 0.0)[:rows]
    grad_taps = jnp.concatenate(
        [flat(roll_columns(grad_own, -1)).astype(BF), flat(grad_own).astype(BF)], axis=1
    )
    first = lax.dot_general(a_rows(rows), grad_taps, over_pixels, preferred_element_type=F32)

    left = lax.broadcasted_iota(jnp.int32, (half, lanes), 1) < half

    part = weight_ref.shape[1]
    me = block_place()

    def keep(block, value):
        done = 0
        while done < half:
            number, at = divmod(block * half + done, part)
            count = min(part - at, half - done)
            weight_ref[number ^ me, at : at + count, :] = value[done : done + count].astype(BF)
            done += count

    def at_left(value):
        return jnp.where(low, value, pltpu.roll(value, half, axis=1))

    def at_right(value):
        return jnp.where(low, pltpu.roll(value, half, axis=1), value)

    centre = []
    for u in range(3):
        top = u * lanes
        for w in range(3):
            across = slice(w * lanes, (w + 1) * lanes)
            keep(
                u * 3 + w,
                jnp.where(low, second[top : top + half, across], second[top + half : top + lanes, across]),
            )
        outer = first[top + half : top + lanes]
        keep(9 + u, jnp.where(left, at_left(outer[:, :lanes]), at_right(outer[:, lanes:])))
        centre.append(first[top : top + half, lanes:])
    keep(12, jnp.where(left, at_left(centre[0]), at_right(centre[1])))
    keep(13, at_left(centre[2]))


def input_kernel(mid_ref, wa_ref, grad_ref):
    rows, own_cols, lanes = grad_ref.shape[0], grad_ref.shape[2], grad_ref.shape[3]
    tall = rows + 1
    by_lanes = (((1,), (1,)), ((), ()))
    grads = flat(mid_ref[...])
    wa = wa_ref[...]
    straight = lax.dot_general(grads, wa[:, lanes:], by_lanes, preferred_element_type=F32)
    shifted = lax.dot_general(grads, wa[:, :lanes], by_lanes, preferred_element_type=F32)

    def taps(u):
        s = slice(u * lanes, (u + 1) * lanes)
        return image(straight[:, s]) + roll_columns(image(shifted[:, s]), -1)

    above, level, below = taps(0), taps(1), taps(2)
    grad_ref[:, 0] = level[:rows, :own_cols].astype(BF)
    grad_ref[:, 1] = (below[:rows, :own_cols] + above[1:tall, :own_cols]).astype(BF)


def unpack_kernel(scale, piece_0, piece_1, piece_2, piece_3, first_ref, second_ref, all_ref):
    half = first_ref.shape[2]
    part = piece_0.shape[0]
    me = block_place()
    for distance, piece in enumerate((piece_0, piece_1, piece_2, piece_3)):
        all_ref[me ^ distance] = piece[...]

    def block(number):
        done, values = 0, []
        while done < half:
            which, at = divmod(number * half + done, part)
            count = min(part - at, half - done)
            values.append(all_ref[which, at : at + count, :].astype(F32) * scale)
            done += count
        return values[0] if len(values) == 1 else jnp.concatenate(values, axis=0)

    for tap in range(9):
        second_ref[tap] = block(tap)
    for u in range(3):
        value = block(9 + u)
        first_ref[3 * u] = value[:, :half]
        first_ref[3 * u + 2] = value[:, half:]
    value = block(12)
    first_ref[1] = value[:, :half]
    first_ref[4] = value[:, half:]
    first_ref[7] = block(13)[:, :half]


def summed_pair(value, axis, size, distance):
    got = lax.ppermute(value, axis, swaps(size, distance))
    return (value.astype(F32) + got.astype(F32)).astype(BF)


def shards(acts, shift, weight_one, weight_two, cotangent, tissue_count, tile_order):
    channels, mids = weight_one.shape[2], weight_one.shape[3]
    height = acts.shape[0]
    lanes = 2 * channels
    pairs = acts.shape[1] // lanes
    rows, cols = height // 2, pairs
    tile_rows, tile_cols = height // TP, 2 * pairs // TP
    out_side = TP // 2
    n_rows, n_tiles = lax.axis_size("rows"), lax.axis_size("tiles")

    whole = pl.BlockSpec(memory_space=pltpu.VMEM)
    in_hbm = pl.BlockSpec(memory_space=pltpu.HBM)
    limit = pltpu.CompilerParams(vmem_limit_bytes=48 << 20)
    half = channels
    n_edges = 1 if n_rows == 2 else 2
    near, edges, place, own_w2, wa, shift_row = pl.pallas_call(
        functools.partial(prepare_kernel, n_rows),
        out_shape=(
            jax.ShapeDtypeStruct((rows, cols, lanes), BF),
            jax.ShapeDtypeStruct((n_edges, 3 * cols, lanes), BF),
            jax.ShapeDtypeStruct((tile_rows, cols, lanes), jnp.int32),
            jax.ShapeDtypeStruct((9 * half, mids), BF),
            jax.ShapeDtypeStruct((3 * lanes, 2 * mids), BF),
            jax.ShapeDtypeStruct((1, mids), F32),
        ),
        in_specs=[in_hbm] * 5,
        out_specs=(whole,) * 6,
        scratch_shapes=[
            pltpu.VMEM((rows, cols, half), BF),
            pltpu.VMEM((3, 3, channels, mids), BF),
            pltpu.SMEM((1, 1, tile_rows * tile_cols), jnp.int32),
            pltpu.SMEM((tile_rows * tile_cols,), jnp.int32),
            pltpu.SemaphoreType.DMA((5,)),
        ],
        compiler_params=limit,
    )(
        *(
            pltpu.with_memory_space_constraint(value, pltpu.HBM)
            for value in (
                tile_order,
                cotangent,
                weight_one,
                weight_two.swapaxes(2, 3).reshape(9 * half, mids),
                shift.reshape(1, mids),
            )
        ),
    )
    other_edges = core_swapped(edges)
    edges, tissue_count = lax.optimization_barrier((edges, tissue_count))
    live = place < tissue_count[0, 0]
    near = jnp.where(live[:, None], near.reshape(tile_rows, -1, cols, lanes), jnp.zeros((), BF))
    near = near.reshape(rows, cols, lanes)
    edges = (edges + other_edges).reshape(n_edges, 3, cols, lanes)
    last = sends_last("rows")
    edge_u = edges[0] if n_rows == 2 else jnp.where(last, edges[1], edges[0])
    edge_u = jnp.where(jnp.where(last, live[-1], live[0]), edge_u, jnp.zeros((), BF))
    edge_u = edge_u.reshape(3 * cols, lanes)
    picture = acts.reshape(height, pairs, lanes)
    edge_a = jnp.where(last, picture[height - 2 :], picture[:2])
    strip = jnp.concatenate([edge_a.reshape(2 * cols, lanes), edge_u], axis=0)
    strip, near, own_w2 = lax.optimization_barrier((strip, near, own_w2))
    before, after = (
        value.reshape(5, cols, lanes)
        for value in before_and_after(*traded(strip, "rows"), "rows")
    )
    far = core_swapped(near)
    other_w2 = core_swapped(own_w2)

    right = sends_last("tiles")
    side = lambda value, count: jnp.where(
        right, value[:, cols - count :], value[:, :count]
    ).reshape(count * value.shape[0], lanes)
    got, got_other = traded(
        jnp.concatenate(
            [
                side(near, 4) + side(far, 4),
                side(picture, 1),
                side(before[:2], 1),
                side(after[:2], 1),
                side(before[2:], 4),
                side(after[2:], 4),
            ],
            axis=0,
        ),
        "tiles",
    )

    part = 14 * half // 4
    mid_grad, weights = pl.pallas_call(
        functools.partial(main_kernel, n_tiles, n_rows),
        out_shape=(
            jax.ShapeDtypeStruct((rows + 1, SLOTS, lanes), BF),
            jax.ShapeDtypeStruct((4, part, lanes), BF),
        ),
        in_specs=[whole] * 11,
        out_specs=(whole, whole),
        scratch_shapes=[
            pltpu.VMEM((rows + 2, 2, SLOTS, lanes), BF),
            pltpu.VMEM((rows + 6, SLOTS, lanes), BF),
            pltpu.VMEM((3 * lanes, 3 * mids), BF),
        ],
        compiler_params=limit,
    )(picture, near, far, own_w2, other_w2, before, after, got, got_other, wa, shift_row)
    input_grad = pl.pallas_call(
        input_kernel,
        out_shape=jax.ShapeDtypeStruct((rows, 2, cols, lanes), BF),
        in_specs=[whole, whole],
        out_specs=whole,
        compiler_params=limit,
    )(mid_grad, wa)

    def from_block(values):
        got = {}
        for d in (1, 2, 3):
            value = values[d - 1]
            for other in got.values():
                value, _ = lax.optimization_barrier((value, other[0]))
            pairs = [
                (t * n_rows + r, (t ^ (d >> 1)) * n_rows + (r ^ (d & 1)))
                for t in range(n_tiles)
                for r in range(n_rows)
            ]
            got[d] = (value, lax.ppermute(value, ("tiles", "rows"), pairs))
        return [got[d][1] for d in (1, 2, 3)]

    one, two, three = from_block([weights[1], weights[2], weights[3]])
    total = (
        (weights[0].astype(F32) + one.astype(F32)) + (two.astype(F32) + three.astype(F32))
    ).astype(BF)
    distance = 2
    while distance < n_rows:
        total = summed_pair(total, "rows", n_rows, distance)
        distance *= 2
    distance = 2
    while distance < n_tiles:
        total = summed_pair(total, "tiles", n_tiles, distance)
        distance *= 2
    pieces = [total] + from_block([total] * 3)

    pixels = n_rows * TISS_MEAN * n_tiles * out_side * out_side
    scale = 1.0 / math.sqrt(pixels)
    first, second = pl.pallas_call(
        functools.partial(unpack_kernel, scale),
        out_shape=(
            jax.ShapeDtypeStruct((9, channels, half), F32),
            jax.ShapeDtypeStruct((9, half, mids), F32),
        ),
        in_specs=[whole] * 4,
        out_specs=(whole, whole),
        scratch_shapes=[pltpu.VMEM((4, part, lanes), BF)],
        compiler_params=limit,
    )(*pieces)
    return (
        input_grad.reshape(height, pairs * lanes),
        first.reshape(3, 3, channels, half),
        second.reshape(3, 3, half, mids).swapaxes(2, 3),
    )


def solution(mesh):
    return jax.shard_map(
        shards,
        mesh=mesh,
        in_specs=(
            P(("groups", "rows"), "tiles"),
            P(),
            P(),
            P(None, None, None, "chan"),
            P(("groups", "rows"), "tiles", "chan"),
            P(("groups", "rows"), "tiles"),
            P(("groups", "rows"), "tiles", None),
        ),
        out_specs=(
            P(("groups", "rows"), "tiles"),
            P("groups", None, None, "chan"),
            P("groups", None, None, "chan"),
        ),
        check_vma=False,
    )
```
